256 devices in a mesh: bucket: 128 (over y, z, x), rep: 2 (over core).
Axes of the slice: x: 4, y: 4, z: 8, core: 2. Of those that a mesh axis runs over, the one named last changes fastest.
Arguments:
- entity_table: bfloat16 [131072, 512], P('bucket'), may hold values from -1.75 to 1.75
- relations: bfloat16 [16, 8, 64, 64], replicated, may hold values from -0.75 to 0.75
- send_rows: int32 [128, 2, 2, 256], P('bucket', 'rep'), may hold values from 0 to 1023, as said below
- send_count: int32 [128, 2, 2, 128], P('bucket', 'rep'), may hold values from 1 to 2, as said below
- heads: int32 [128, 2, 2, 1, 512], P('bucket', 'rep'), may hold values from 0 to 255, as said below
- tails: int32 [128, 2, 2, 1, 512], P('bucket', 'rep'), may hold values from 0 to 255, as said below
- negatives: int32 [128, 2, 2, 1, 1000], P('bucket', 'rep'), may hold values from 0 to 255, as said below
- span_rel: int32 [128, 2, 2, 1], P('bucket', 'rep'), may hold values from 0 to 15
Outputs:
- entity_grad: float32 [131072, 512], P('bucket')
- relation_grad: float32 [16, 8, 64, 64], replicated
The draws below stay inside these ranges and needn't reach their ends.
Inputs may be any that keep to these rules, and one draw needn't show every extreme that they name: send_count[s, r, k, d] rows go from device (s, r) to bucket index d for edge bucket k; for every r and k one destination, drawn from the seed, receives exactly 2 rows from every source. The first entries of send_rows[s, r, k] list the rows for destination 0, then for destination 1 and so on, send_count[s, r, k, d] of them each; later entries are unused. `heads`: a slot s * 2 + j named on device (d, r) for bucket k always has j < send_count[s, r, k, d]. `tails`: a slot s * 2 + j named on device (d, r) for bucket k always has j < send_count[s, r, k, d]. `negatives`: a slot s * 2 + j named on device (d, r) for bucket k always has j < send_count[s, r, k, d].
All inputs are finite; a program needn't handle non-finite values.
Results may differ from the reference program's by a relative error of at most 0.009.
Values may be sent and summed in bfloat16 or wider, within the bound.
No kernel may reach another device: no remote copies, remote signals or barrier semaphores. Data moves between devices by JAX's collectives and lax.ppermute only.
A program may use at most 64 MiB of HBM per device.

```python
import jax
import jax.numpy as jnp
from jax import lax

D = 512
BLK = 64
REL = 16
ENT_DEV = 1024
SLOTS_DEV = 256
NB = 2
SPANS = 1
SPAN = 512
NEG = 1000
NBLK = 8
BUCKETS = 128
REPLICAS = 2
CAP = 2
ENTITIES = 131072


def counts_table(key):
    first = jax.random.fold_in(key, 11)
    second = jax.random.fold_in(key, 12)
    base = jax.random.randint(first, (BUCKETS, REPLICAS, NB, BUCKETS), 1, CAP + 1)
    chosen = jax.random.randint(second, (REPLICAS, NB), 0, BUCKETS)
    dest = jnp.arange(BUCKETS)
    filled = dest[None, None, None, :] == chosen[None, :, :, None]
    return jnp.where(filled, CAP, base).astype(jnp.int32)


def pick_slots(key, label, length):
    counts_all = counts_table(key)
    by_dest = jnp.transpose(counts_all, (3, 1, 2, 0))
    source = jax.random.randint(jax.random.fold_in(key, label), (BUCKETS, REPLICAS, NB, SPANS * length), 0, BUCKETS)
    limits = jnp.take_along_axis(by_dest, source, axis=3)
    offset_key = jax.random.fold_in(key, label + 1)
    within = jax.random.randint(offset_key, (BUCKETS, REPLICAS, NB, SPANS * length), 0, limits)
    slots_all = source * CAP + within
    return slots_all.reshape(BUCKETS, REPLICAS, NB, SPANS, length).astype(jnp.int32)


def draw_send_count(key, part):
    return counts_table(key)


def draw_send_rows(key, part):
    return jax.random.randint(jax.random.fold_in(key, 21), (BUCKETS, REPLICAS, NB, SLOTS_DEV), 0, ENT_DEV).astype(jnp.int32)


def draw_heads(key, part):
    return pick_slots(key, 31, SPAN)


def draw_tails(key, part):
    return pick_slots(key, 41, SPAN)


def draw_negatives(key, part):
    return pick_slots(key, 51, NEG)


def place_ends(values, stream_key, smallest, high):
    index_at = [jax.random.randint(jax.random.fold_in(stream_key, axis), (), 0, length) for axis, length in enumerate(values.shape)]
    longest = values.shape.index(max(values.shape))
    beside = index_at[:longest] + [(index_at[longest] + 1) % values.shape[longest]] + index_at[longest + 1:]
    return values.at[tuple(index_at)].set(smallest).at[tuple(beside)].set(high)


def shard_levels(rng, extent, shards, smallest, top_value):
    loudness, own = 1.0, jax.random.fold_in(rng, 6)
    for position, shards_of in shards:
        heights = jnp.exp(jax.random.uniform(jax.random.fold_in(own, position), (shards_of,), jnp.float32, smallest / len(shards), top_value / len(shards)))
        loudness = loudness * jnp.repeat(heights, extent[position] // shards_of).reshape([-1 if axis == position else 1 for axis in range(len(extent))])
    return loudness


def centred(key, shape, width, reach, shards=(), held_as=jnp.bfloat16):
    entries = jax.random.normal(key, shape, jnp.float32) * width
    if len(shards) > 0:
        entries = shard_levels(key, shape, shards, -0.22, 0.18) * entries
    return jnp.clip(entries, min=-reach, max=reach).astype(held_as)


def setup_inputs(seed: int = 0) -> dict:
    seeds = jax.random.split(jax.random.key(seed), 9)
    return {
        "entity_table": centred(seeds[0], (ENTITIES, D), 0.3, 1.75, ((0, 128),)),
        "relations": centred(seeds[1], (REL, NBLK, BLK, BLK), BLK ** -0.5, 0.75),
        "send_rows": draw_send_rows(jax.random.fold_in(seeds[8], 71), 0),
        "send_count": draw_send_count(jax.random.fold_in(seeds[8], 71), 0),
        "heads": draw_heads(jax.random.fold_in(seeds[8], 71), 0),
        "tails": draw_tails(jax.random.fold_in(seeds[8], 71), 0),
        "negatives": draw_negatives(jax.random.fold_in(seeds[8], 71), 0),
        "span_rel": place_ends(jax.random.randint(seeds[7], (BUCKETS, REPLICAS, NB, SPANS), 0, REL), jax.random.fold_in(seeds[7], 1), 0, REL - 1).astype(jnp.int32),
    }


def span_grads(fetched, rel_mat, head_ids, tail_ids, neg_ids):
    edge_count = head_ids.shape[0]
    head_rows = fetched[head_ids]
    tail_rows = fetched[tail_ids]
    neg_rows = fetched[neg_ids]
    head_blocks = head_rows.reshape(edge_count, NBLK, BLK).astype(jnp.float32)
    rel_float = rel_mat.astype(jnp.float32)
    rotated = jnp.einsum("ebi,bio->ebo", head_blocks, rel_float).reshape(edge_count, D).astype(jnp.bfloat16)
    positive = jnp.sum(rotated.astype(jnp.float32) * tail_rows.astype(jnp.float32), axis=1)
    negative = jnp.dot(rotated, neg_rows.T, preferred_element_type=jnp.float32)
    pos_grad = -jax.nn.sigmoid(-positive)
    neg_weight = (jax.nn.sigmoid(negative) / NEG).astype(jnp.bfloat16)
    grad_tail = pos_grad[:, None] * rotated.astype(jnp.float32)
    grad_negative = jnp.dot(neg_weight.T, rotated, preferred_element_type=jnp.float32)
    grad_rotated = (pos_grad[:, None] * tail_rows.astype(jnp.float32)
                    + jnp.dot(neg_weight, neg_rows, preferred_element_type=jnp.float32)).astype(jnp.bfloat16)
    grad_blocks = grad_rotated.reshape(edge_count, NBLK, BLK).astype(jnp.float32)
    grad_head = jnp.einsum("ebo,bio->ebi", grad_blocks, rel_float).reshape(edge_count, D)
    grad_rel = jnp.einsum("ebi,ebo->bio", head_blocks, grad_blocks)
    return grad_head, grad_tail, grad_negative, grad_rel


def reference(entity_table, relations, send_rows, send_count, heads, tails, negatives, span_rel):
    owned_rows = entity_table.reshape(BUCKETS, ENT_DEV, D)
    offsets = jnp.cumsum(send_count, axis=3) - send_count
    column = jnp.arange(CAP, dtype=jnp.int32)
    sources = jnp.arange(BUCKETS, dtype=jnp.int32)[:, None]

    def receiver(totals, device_id):
        entity_sum, relation_sum = totals
        dest_id = device_id // REPLICAS
        rep_id = device_id % REPLICAS
        for bucket in range(NB):
            counts_k = send_count[:, rep_id, bucket, dest_id]
            starts = offsets[:, rep_id, bucket, dest_id]
            flat_pos = jnp.clip(starts[:, None] + column[None, :], 0, SLOTS_DEV - 1).astype(jnp.int32)
            row_ids = jnp.take_along_axis(send_rows[:, rep_id, bucket, :], flat_pos, axis=1)
            is_valid = column[None, :] < counts_k[:, None]
            gathered = owned_rows[sources, row_ids]
            fetched = jnp.where(is_valid[:, :, None], gathered, jnp.zeros((), jnp.bfloat16))
            fetched = fetched.astype(jnp.bfloat16).reshape(SLOTS_DEV, D)
            slot_grad = jnp.zeros((SLOTS_DEV, D), jnp.float32)
            for span in range(SPANS):
                rel_id = span_rel[dest_id, rep_id, bucket, span]
                head_ids = heads[dest_id, rep_id, bucket, span]
                tail_ids = tails[dest_id, rep_id, bucket, span]
                neg_ids = negatives[dest_id, rep_id, bucket, span]
                grad_head, grad_tail, grad_negative, grad_rel = span_grads(
                    fetched, relations[rel_id], head_ids, tail_ids, neg_ids)
                slot_grad = slot_grad.at[head_ids].add(grad_head)
                slot_grad = slot_grad.at[tail_ids].add(grad_tail)
                slot_grad = slot_grad.at[neg_ids].add(grad_negative)
                relation_sum = relation_sum.at[rel_id].add(grad_rel)
            rounded = lax.optimization_barrier(slot_grad.astype(jnp.bfloat16)).astype(jnp.float32)
            masked = jnp.where(is_valid[:, :, None], rounded.reshape(BUCKETS, CAP, D), jnp.zeros((), jnp.float32))
            entity_sum = entity_sum.at[sources, row_ids].add(masked)
        return (entity_sum, relation_sum), None

    start = (jnp.zeros((BUCKETS, ENT_DEV, D), jnp.float32), jnp.zeros((REL, NBLK, BLK, BLK), jnp.float32))
    totals, unused = lax.scan(receiver, start, jnp.arange(BUCKETS * REPLICAS, dtype=jnp.int32))
    return totals[0].reshape(ENTITIES, D), totals[1]
```

```python
import functools

import jax
import jax.numpy as jnp
from jax import lax
from jax.experimental import pallas as pl
from jax.experimental.pallas import tpu as pltpu
from jax.sharding import PartitionSpec as P

F32 = jnp.float32
BF16 = jnp.bfloat16
VMEM = pl.BlockSpec(memory_space=pltpu.VMEM)


def iota(shape, dim):
    return lax.broadcasted_iota(jnp.int32, shape, dim)


def dot(a, b, ca=1, cb=0):
    return lax.dot_general(a, b, (((ca,), (cb,)), ((), ())), preferred_element_type=F32)


def onehot(mask):
    return jnp.where(mask, 1.0, 0.0).astype(BF16)


def unpack_matrix():
    g = iota((256, 256), 0)
    p = iota((256, 256), 1)
    return onehot(p == (g & 31) * 8 + (g >> 5))


def pack_matrix():
    p = iota((256, 256), 0)
    g = iota((256, 256), 1)
    return onehot(p == (g & 31) * 8 + (g >> 5))


def slot_row(ids):
    return ((ids >> 6) << 6) | ((ids & 1) << 5) | ((ids >> 1) & 31)


def pack_slots(read, write):
    matrix = pack_matrix()
    for b in range(4):
        rows = jnp.concatenate(
            [read(k, b)[:, h * 256 : h * 256 + 256] for h in range(2) for k in range(2)], axis=0
        )
        write(b, dot(matrix, rows).astype(BF16))


def unpack_slots(read, write):
    matrix = unpack_matrix()
    for b in range(4):
        rows = dot(matrix, read(b)).astype(BF16)
        for h in range(2):
            for k in range(2):
                start = h * 128 + k * 64
                write(k, b, h, rows[start : start + 64])


def send_kernel(rows_ref, count_ref, table_ref, packed_ref, ids_ref, slots):
    table = table_ref[...]
    row = iota((256, 128), 0)
    chip = (row >> 6) * 32 + (row & 31)
    other = iota((256, 128), 1)
    column = (iota((256, 1), 0) >> 5) & 1
    flat = iota((256, 256), 1)
    entity = iota((256, table.shape[0]), 1)
    ids_ref[...] = jnp.zeros_like(ids_ref)
    for k in range(2):
        counts = count_ref[k : k + 1, :].astype(F32)
        start = jnp.sum(jnp.where(other < chip, counts, 0.0), axis=1, keepdims=True)
        count = jnp.sum(jnp.where(other == chip, counts, 0.0), axis=1, keepdims=True)
        position = start.astype(jnp.int32) + column
        names = rows_ref[k : k + 1, :].astype(F32)
        ids = jnp.sum(jnp.where(flat == position, names, 0.0), axis=1, keepdims=True)
        ids = jnp.where(column < count.astype(jnp.int32), ids, -1.0)
        ids_ref[k : k + 1, :] = jnp.transpose(jnp.broadcast_to(ids, (256, 128)))[0:1, :]
        chosen = onehot(entity == ids.astype(jnp.int32))
        slots[k] = dot(chosen, table).astype(BF16)

    def write(b, rows):
        packed_ref[b * 256 : b * 256 + 256, :] = rows

    pack_slots(lambda k, b: slots[k, b * 64 : b * 64 + 64, :], write)


def step_kernel(
    rel_ref, packed_ref, first_ref, second_ref, heads_ref, tails_ref, neg_ref, out_ref, slots, diag, grads, partial
):
    def write(k, b, h, rows):
        slots[k, b * 64 : b * 64 + 64, h * 256 : h * 256 + 256] = rows

    unpack_slots(lambda b: packed_ref[b * 256 : b * 256 + 256, :], write)
    neg_count = neg_ref.shape[1]
    lane_block = iota((64, 256), 1) >> 6
    for k in range(2):
        relation = (first_ref, second_ref)[k]
        for c in range(2):
            for j in range(4):
                place = onehot(iota((64, 256), 1) == iota((64, 256), 0) + 64 * j)
                diag[k, c, 64 * j : 64 * j + 64, :] = dot(relation[0, 4 * c + j], place).astype(BF16)
        rows = slots[k]
        rotated = jnp.concatenate(
            [dot(rows[:, c * 256 : c * 256 + 256], diag[k, c]) for c in range(2)], axis=1
        ).astype(BF16)
        slot = iota((256, 512), 0)
        at_head = onehot(slot == slot_row(heads_ref[k : k + 1, :]))
        at_tail = onehot(slot == slot_row(tails_ref[k : k + 1, :]))
        edges = dot(at_head, at_tail, 1, 1)
        head_edges = jnp.sum(edges, axis=1, keepdims=True)
        at_neg = onehot(iota((256, neg_count), 0) == slot_row(neg_ref[k : k + 1, :]))
        times = dot(jnp.ones((8, neg_count), BF16), at_neg, 1, 1)[0:1, :]
        score = dot(rotated, rows, 1, 1)
        small = jnp.exp(-jnp.abs(score))
        big_side = 1.0 / (1.0 + small)
        small_side = small * big_side
        sigmoid = jnp.where(score >= 0, big_side, small_side)
        sigmoid_neg = jnp.where(score >= 0, small_side, big_side)
        weight = ((head_edges * times) * sigmoid / neg_count - edges * sigmoid_neg).astype(BF16)
        grad_rotated = dot(weight, rows).astype(BF16)
        grad_other = dot(weight, rotated, 0, 0)
        for c in range(2):
            lanes = slice(c * 256, c * 256 + 256)
            grad_head = dot(grad_rotated[:, lanes], diag[k, c], 1, 1)
            grads[k, :, lanes] = (grad_head + grad_other[:, lanes]).astype(BF16)
            outer = dot(rows[:, lanes], grad_rotated[:, lanes], 0, 0)
            total = jnp.zeros((64, 256), F32)
            for j in range(4):
                total = jnp.where(lane_block == j, outer[64 * j : 64 * j + 64, :], total)
            partial[k, :, lanes] = total.astype(BF16)

    def write_packed(b, rows):
        out_ref[b * 256 : b * 256 + 256, 0:256] = rows

    pack_slots(lambda k, b: grads[k, b * 64 : b * 64 + 64, :], write_packed)
    p = iota((256, 128), 0)
    g = iota((256, 128), 1)
    piece = p & 3
    source = ((p >> 2) & 1) * 64 + (((p >> 3) & 1) * 2 + piece) * 16 + (p >> 4)
    spread = onehot((g == source) & (piece < 2))
    named = jnp.where(((p >> 2) & 1) == 0, rel_ref[0], rel_ref[1]).astype(F32)
    for b in range(4):
        rows = jnp.concatenate(
            [partial[k, b * 16 : b * 16 + 16, q * 128 : q * 128 + 128] for k in range(2) for q in range(4)], axis=0
        )
        out_ref[b * 256 : b * 256 + 256, 256:384] = jnp.where(piece == 2, named, dot(spread, rows)).astype(BF16)


def relation_kernel(rep_ref, own_ref, peer_ref, out_ref):
    matrix = unpack_matrix()
    lane = iota((128, 128), 1)
    totals = [jnp.zeros((128, 128), F32) for q in range(2)]
    for ref in (own_ref, peer_ref):
        blocks = [dot(matrix, ref[b * 256 : b * 256 + 256, :]) for b in range(4)]

        def piece(index):
            return jnp.concatenate([rows[index * 32 : index * 32 + 32] for rows in blocks], axis=0)

        for k in range(2):
            chosen = onehot(lane == piece(4 * k + 2).astype(jnp.int32))
            for q in range(2):
                totals[q] = totals[q] + dot(chosen, piece(4 * k + q).astype(BF16), 0, 0)
    mine = jnp.where(rep_ref[0] == 0, totals[0], totals[1])[0:16].astype(BF16)
    for d in range(128):
        out_ref[d * 16 : d * 16 + 16, :] = mine


def scatter_kernel(own_ref, peer_ref, own_ids, peer_ids, out_ref, rows_ref):
    @pl.when(pl.program_id(0) == 0)
    def _():
        for r, ref in enumerate((own_ref, peer_ref)):

            def write(k, b, h, rows):
                start = (r * 2 + k) * 256 + b * 64
                rows_ref[start : start + 64, h * 256 : h * 256 + 256] = rows

            unpack_slots(lambda b: ref[b * 256 : b * 256 + 256, :], write)

    base = pl.program_id(0) * 256
    entity = iota((256, 256), 0) + base
    total = jnp.zeros(out_ref.shape, F32)
    for r, ref in enumerate((own_ids, peer_ids)):
        for k in range(2):
            start = (r * 2 + k) * 256
            hit = onehot(entity == ref[k : k + 1, :].astype(jnp.int32))
            total = total + dot(hit, rows_ref[start : start + 256, :])
    out_ref[...] = total


def assemble_kernel(rep_ref, own_ref, peer_ref, out_ref):
    g = iota((256, 256), 0)
    p = iota((256, 256), 1)
    matrix = onehot(p == ((g & 7) * 2 + ((g >> 3) & 1)) * 16 + (g >> 4))
    first = rep_ref[0] == 0
    for d in range(8):
        own = dot(matrix, own_ref[d * 256 : d * 256 + 256, :])
        peer = dot(matrix, peer_ref[d * 256 : d * 256 + 256, :])
        for q in range(2):
            rows = jnp.where(first, own, peer) if q == 0 else jnp.where(first, peer, own)
            rows = rows.reshape(16, 2, 8, 128)
            for half in range(2):
                block = half * 4 + q * 2
                out_ref[:, block, d * 8 : d * 8 + 8, :] = rows[:, half, :, 0:64]
                out_ref[:, block + 1, d * 8 : d * 8 + 8, :] = rows[:, half, :, 64:128]


def body(entity_table, relations, send_rows, send_count, heads, tails, negatives, span_rel):
    entities, width = entity_table.shape
    chips = send_count.shape[3]
    rep = lax.axis_index("rep").astype(jnp.int32).reshape(1)
    swap = [(0, 1), (1, 0)]

    packed, ids = pl.pallas_call(
        send_kernel,
        out_shape=(jax.ShapeDtypeStruct((chips * 8, 256), BF16), jax.ShapeDtypeStruct((8, 256), F32)),
        in_specs=[VMEM] * 3,
        out_specs=(VMEM, VMEM),
        scratch_shapes=[pltpu.VMEM((2, 256, width), BF16)],
        name="send_rows",
    )(send_rows[0, 0], send_count[0, 0], entity_table)
    peer_ids = lax.ppermute(ids, "rep", swap)

    received = lax.all_to_all(packed.reshape(chips, 8, 256), "bucket", 0, 0, tiled=True)

    rel_ids = span_rel.reshape(2)
    whole = lambda shape: pl.BlockSpec(shape, lambda i, rel: (0,) * len(shape))
    relation_spec = lambda k: pl.BlockSpec((1, 8, 64, 64), lambda i, rel: (rel[k], 0, 0, 0))
    returned = pl.pallas_call(
        step_kernel,
        out_shape=jax.ShapeDtypeStruct((chips * 8, 384), BF16),
        grid_spec=pltpu.PrefetchScalarGridSpec(
            num_scalar_prefetch=1,
            grid=(1,),
            in_specs=[
                whole((chips * 8, 256)),
                relation_spec(0),
                relation_spec(1),
                whole((2, heads.shape[4])),
                whole((2, tails.shape[4])),
                whole((2, negatives.shape[4])),
            ],
            out_specs=whole((chips * 8, 384)),
            scratch_shapes=[
                pltpu.VMEM((2, 256, width), BF16),
                pltpu.VMEM((2, 2, 256, 256), BF16),
                pltpu.VMEM((2, 256, width), BF16),
                pltpu.VMEM((2, 64, width), BF16),
            ],
        ),
        name="train_step",
    )(
        rel_ids,
        received.reshape(chips * 8, 256),
        relations,
        relations,
        heads.reshape(2, -1),
        tails.reshape(2, -1),
        negatives.reshape(2, -1),
    )

    own = lax.all_to_all(returned.reshape(chips, 8, 384), "bucket", 0, 0, tiled=True).reshape(chips * 8, 384)
    peer = lax.ppermute(own, "rep", swap)

    slice_spec = pl.BlockSpec((chips * 8, 128), lambda i, rep: (0, 2))
    slices = pl.pallas_call(
        relation_kernel,
        out_shape=jax.ShapeDtypeStruct((chips * 16, 128), BF16),
        grid_spec=pltpu.PrefetchScalarGridSpec(
            num_scalar_prefetch=1,
            grid=(1,),
            in_specs=[slice_spec, slice_spec],
            out_specs=pl.BlockSpec((chips * 16, 128), lambda i, rep: (0, 0)),
        ),
        name="sum_relations",
    )(rep, own, peer)
    gathered = lax.all_to_all(slices.reshape(chips, 16, 128), "bucket", 0, 0, tiled=True).reshape(chips * 16, 128)

    chunk = 256
    rows_spec = pl.BlockSpec((chips * 8, 256), lambda i: (0, 0))
    ids_spec = pl.BlockSpec((8, 256), lambda i: (0, 0))
    entity_grad = pl.pallas_call(
        scatter_kernel,
        out_shape=jax.ShapeDtypeStruct((entities, width), F32),
        grid=(entities // chunk,),
        in_specs=[rows_spec, rows_spec, ids_spec, ids_spec],
        out_specs=pl.BlockSpec((chunk, width), lambda i: (i, 0)),
        scratch_shapes=[pltpu.VMEM((1024, width), BF16)],
        name="scatter_rows",
    )(own, peer, ids, peer_ids)

    peer_gathered = lax.ppermute(gathered, "rep", swap)
    full = lambda i, rep: (0, 0)
    relation_grad = pl.pallas_call(
        assemble_kernel,
        out_shape=jax.ShapeDtypeStruct(relations.shape, F32),
        grid_spec=pltpu.PrefetchScalarGridSpec(
            num_scalar_prefetch=1,
            grid=(1,),
            in_specs=[pl.BlockSpec((chips * 16, 128), full)] * 2,
            out_specs=pl.BlockSpec(relations.shape, lambda i, rep: (0, 0, 0, 0)),
        ),
        compiler_params=pltpu.CompilerParams(vmem_limit_bytes=48 << 20),
        name="assemble_relations",
    )(rep, gathered, peer_gathered)
    return entity_grad, relation_grad


def solution(mesh):
    return jax.shard_map(
        body,
        mesh=mesh,
        in_specs=(
            P("bucket", None),
            P(),
            P("bucket", "rep", None, None),
            P("bucket", "rep", None, None),
            P("bucket", "rep", None, None, None),
            P("bucket", "rep", None, None, None),
            P("bucket", "rep", None, None, None),
            P("bucket", "rep", None, None),
        ),
        out_specs=(P("bucket", None), P()),
        check_vma=False,
    )
```

```python
import functools

import jax
import jax.numpy as jnp
from jax import lax
from jax.experimental import pallas as pl
from jax.experimental.pallas import tpu as pltpu
from jax.sharding import PartitionSpec as P

F32 = jnp.float32
BF16 = jnp.bfloat16
VMEM = pl.BlockSpec(memory_space=pltpu.VMEM)


def iota(shape, dim):
    return lax.broadcasted_iota(jnp.int32, shape, dim)


def dot(a, b, ca=1, cb=0):
    return lax.dot_general(a, b, (((ca,), (cb,)), ((), ())), preferred_element_type=F32)


def onehot(mask):
    return jnp.where(mask, 1.0, 0.0).astype(BF16)


def unpack_matrix():
    g = iota((256, 256), 0)
    p = iota((256, 256), 1)
    return onehot(p == (g & 31) * 8 + (g >> 5))


def pack_matrix():
    p = iota((256, 256), 0)
    g = iota((256, 256), 1)
    return onehot(p == (g & 31) * 8 + (g >> 5))


def slot_row(ids):
    return ((ids >> 6) << 6) | ((ids & 1) << 5) | ((ids >> 1) & 31)


def pack_slots(read, write):
    matrix = pack_matrix()
    for b in range(4):
        rows = jnp.concatenate(
            [read(k, b)[:, h * 256 : h * 256 + 256] for h in range(2) for k in range(2)], axis=0
        )
        write(b, dot(matrix, rows).astype(BF16))


def unpack_slots(read, write):
    matrix = unpack_matrix()
    for b in range(4):
        rows = dot(matrix, read(b)).astype(BF16)
        for h in range(2):
            for k in range(2):
                start = h * 128 + k * 64
                write(k, b, h, rows[start : start + 64])


def send_kernel(rows_ref, count_ref, table_ref, packed_ref, ids_ref, slots):
    table = table_ref[...]
    row = iota((256, 128), 0)
    chip = (row >> 6) * 32 + (row & 31)
    other = iota((256, 128), 1)
    column = (iota((256, 1), 0) >> 5) & 1
    flat = iota((256, 256), 1)
    entity = iota((256, table.shape[0]), 1)
    ids_ref[...] = jnp.zeros_like(ids_ref)
    for k in range(2):
        counts = count_ref[k : k + 1, :].astype(F32)
        start = jnp.sum(jnp.where(other < chip, counts, 0.0), axis=1, keepdims=True)
        count = jnp.sum(jnp.where(other == chip, counts, 0.0), axis=1, keepdims=True)
        position = start.astype(jnp.int32) + column
        names = rows_ref[k : k + 1, :].astype(F32)
        ids = jnp.sum(jnp.where(flat == position, names, 0.0), axis=1, keepdims=True)
        ids = jnp.where(column < count.astype(jnp.int32), ids, -1.0)
        ids_ref[k : k + 1, :] = jnp.transpose(jnp.broadcast_to(ids, (256, 128)))[0:1, :]
        chosen = onehot(entity == ids.astype(jnp.int32))
        slots[k] = dot(chosen, table).astype(BF16)

    def write(b, rows):
        packed_ref[b * 256 : b * 256 + 256, :] = rows

    pack_slots(lambda k, b: slots[k, b * 64 : b * 64 + 64, :], write)


def step_kernel(
    rel_ref, packed_ref, first_ref, second_ref, heads_ref, tails_ref, neg_ref, out_ref, slots, diag, grads, partial
):
    def write(k, b, h, rows):
        slots[k, b * 64 : b * 64 + 64, h * 256 : h * 256 + 256] = rows

    unpack_slots(lambda b: packed_ref[b * 256 : b * 256 + 256, :], write)
    neg_count = neg_ref.shape[1]
    lane_block = iota((64, 256), 1) >> 6
    for k in range(2):
        relation = (first_ref, second_ref)[k]
        for c in range(2):
            for j in range(4):
                place = onehot(iota((64, 256), 1) == iota((64, 256), 0) + 64 * j)
                diag[k, c, 64 * j : 64 * j + 64, :] = dot(relation[0, 4 * c + j], place).astype(BF16)
        rows = slots[k]
        rotated = jnp.concatenate(
            [dot(rows[:, c * 256 : c * 256 + 256], diag[k, c]) for c in range(2)], axis=1
        ).astype(BF16)
        slot = iota((256, 512), 0)
        at_head = onehot(slot == slot_row(heads_ref[k : k + 1, :]))
        at_tail = onehot(slot == slot_row(tails_ref[k : k + 1, :]))
        edges = dot(at_head, at_tail, 1, 1)
        head_edges = jnp.sum(edges, axis=1, keepdims=True)
        at_neg = onehot(iota((256, neg_count), 0) == slot_row(neg_ref[k : k + 1, :]))
        times = dot(jnp.ones((8, neg_count), BF16), at_neg, 1, 1)[0:1, :]
        score = dot(rotated, rows, 1, 1)
        small = jnp.exp(-jnp.abs(score))
        big_side = 1.0 / (1.0 + small)
        small_side = small * big_side
        sigmoid = jnp.where(score >= 0, big_side, small_side)
        sigmoid_neg = jnp.where(score >= 0, small_side, big_side)
        weight = ((head_edges * times) * sigmoid / neg_count - edges * sigmoid_neg).astype(BF16)
        grad_rotated = dot(weight, rows).astype(BF16)
        grad_other = dot(weight, rotated, 0, 0)
        for c in range(2):
            lanes = slice(c * 256, c * 256 + 256)
            grad_head = dot(grad_rotated[:, lanes], diag[k, c], 1, 1)
            grads[k, :, lanes] = (grad_head + grad_other[:, lanes]).astype(BF16)
            outer = dot(rows[:, lanes], grad_rotated[:, lanes], 0, 0)
            total = jnp.zeros((64, 256), F32)
            for j in range(4):
                total = jnp.where(lane_block == j, outer[64 * j : 64 * j + 64, :], total)
            partial[k, :, lanes] = total.astype(BF16)

    def write_packed(b, rows):
        out_ref[b * 256 : b * 256 + 256, 0:256] = rows

    pack_slots(lambda k, b: grads[k, b * 64 : b * 64 + 64, :], write_packed)
    p = iota((256, 128), 0)
    g = iota((256, 128), 1)
    piece = p & 3
    source = ((p >> 2) & 1) * 64 + (((p >> 3) & 1) * 2 + piece) * 16 + ((p >> 4) & 1) * 8 + (p >> 5)
    spread = onehot((g == source) & (piece < 2))
    named = jnp.where(((p >> 2) & 1) == 0, rel_ref[0], rel_ref[1]).astype(F32)
    for b in range(4):
        rows = jnp.concatenate(
            [partial[k, b * 16 : b * 16 + 16, q * 128 : q * 128 + 128] for k in range(2) for q in range(4)], axis=0
        )
        out_ref[b * 256 : b * 256 + 256, 256:384] = jnp.where(piece == 2, named, dot(spread, rows)).astype(BF16)


def relation_kernel(rep_ref, own_ref, keep_ref, give_ref):
    matrix = unpack_matrix()
    lane = iota((128, 128), 1)
    totals = [jnp.zeros((128, 128), F32) for q in range(2)]
    blocks = [dot(matrix, own_ref[b * 256 : b * 256 + 256, :]) for b in range(4)]

    def piece(index):
        return jnp.concatenate([rows[index * 32 : index * 32 + 32] for rows in blocks], axis=0)

    for k in range(2):
        chosen = onehot(lane == piece(4 * k + 2).astype(jnp.int32))
        for q in range(2):
            totals[q] = totals[q] + dot(chosen, piece(4 * k + q).astype(BF16), 0, 0)
    first = rep_ref[0] == 0
    keep_ref[...] = jnp.where(first, totals[0], totals[1])[0:16]
    give_ref[...] = jnp.where(first, totals[1], totals[0])[0:16]


def scatter_kernel(own_ref, peer_ref, own_ids, peer_ids, out_ref, rows_ref):
    @pl.when(pl.program_id(0) == 0)
    def _():
        for r, ref in enumerate((own_ref, peer_ref)):

            def write(k, b, h, rows):
                start = (r * 2 + k) * 256 + b * 64
                rows_ref[start : start + 64, h * 256 : h * 256 + 256] = rows

            unpack_slots(lambda b: ref[b * 256 : b * 256 + 256, :], write)

    base = pl.program_id(0) * 256
    entity = iota((256, 256), 0) + base
    total = jnp.zeros(out_ref.shape, F32)
    for r, ref in enumerate((own_ids, peer_ids)):
        for k in range(2):
            start = (r * 2 + k) * 256
            hit = onehot(entity == ref[k : k + 1, :].astype(jnp.int32))
            total = total + dot(hit, rows_ref[start : start + 256, :])
    out_ref[...] = total


def assemble_kernel(rep_ref, own_ref, peer_ref, out_ref):
    g = iota((256, 256), 0)
    p = iota((256, 256), 1)
    matrix = onehot(p == ((g >> 3) & 1) * 128 + (g & 7) * 16 + (g >> 4))
    first = rep_ref[0] == 0
    for y in range(4):
        for m in range(2):
            rows = slice((y * 2 + m) * 256, (y * 2 + m) * 256 + 256)
            own = dot(matrix, own_ref[rows, :])
            peer = dot(matrix, peer_ref[rows, :])
            for q in range(2):
                part = jnp.where(first, own, peer) if q == 0 else jnp.where(first, peer, own)
                part = part.reshape(16, 2, 8, 128)
                for half in range(2):
                    block = half * 4 + q * 2
                    out_ref[:, block, (y * 2 + m) * 8 : (y * 2 + m) * 8 + 8, :] = part[:, half, :, 0:64]
                    out_ref[:, block + 1, (y * 2 + m) * 8 : (y * 2 + m) * 8 + 8, :] = part[:, half, :, 64:128]


def chip(y, z, x):
    return (y * 8 + z) * 4 + x


ALONG_Z = [[chip(y, z, x) for z in range(8)] for y in range(4) for x in range(4)]
IN_PLANE = [[chip(y, z, x) for y in range(4) for x in range(4)] for z in range(8)]


def gather_among(rows, groups):
    count = len(groups[0])
    spread = jnp.broadcast_to(rows[None], (count,) + rows.shape)
    out = lax.all_to_all(spread, "bucket", 0, 0, axis_index_groups=groups, tiled=True)
    return out.reshape(count * rows.shape[0], rows.shape[1])


def limit(mib):
    return pltpu.CompilerParams(vmem_limit_bytes=mib << 20)


def body(entity_table, relations, send_rows, send_count, heads, tails, negatives, span_rel):
    entities, width = entity_table.shape
    chips = send_count.shape[3]
    rep = lax.axis_index("rep").astype(jnp.int32).reshape(1)
    swap = [(0, 1), (1, 0)]

    packed, ids = pl.pallas_call(
        send_kernel,
        out_shape=(jax.ShapeDtypeStruct((chips * 8, 256), BF16), jax.ShapeDtypeStruct((8, 256), F32)),
        in_specs=[VMEM] * 3,
        out_specs=(VMEM, VMEM),
        scratch_shapes=[pltpu.VMEM((2, 256, width), BF16)],
        compiler_params=limit(16),
        name="send_rows",
    )(send_rows[0, 0], send_count[0, 0], entity_table)
    peer_ids = lax.ppermute(ids, "rep", swap)

    received = lax.all_to_all(packed.reshape(chips, 8, 256), "bucket", 0, 0, tiled=True).reshape(chips * 8, 256)
    received, peer_ids = lax.optimization_barrier((received, peer_ids))

    rel_ids = span_rel.reshape(2)
    whole = lambda shape: pl.BlockSpec(shape, lambda i, rel: (0,) * len(shape))
    relation_spec = lambda k: pl.BlockSpec((1, 8, 64, 64), lambda i, rel: (rel[k], 0, 0, 0))
    returned = pl.pallas_call(
        step_kernel,
        out_shape=jax.ShapeDtypeStruct((chips * 8, 384), BF16),
        grid_spec=pltpu.PrefetchScalarGridSpec(
            num_scalar_prefetch=1,
            grid=(1,),
            in_specs=[
                whole((chips * 8, 256)),
                relation_spec(0),
                relation_spec(1),
                whole((2, heads.shape[4])),
                whole((2, tails.shape[4])),
                whole((2, negatives.shape[4])),
            ],
            out_specs=whole((chips * 8, 384)),
            scratch_shapes=[
                pltpu.VMEM((2, 256, width), BF16),
                pltpu.VMEM((2, 2, 256, 256), BF16),
                pltpu.VMEM((2, 256, width), BF16),
                pltpu.VMEM((2, 64, width), BF16),
            ],
        ),
        compiler_params=limit(24),
        name="train_step",
    )(
        rel_ids,
        received,
        relations,
        relations,
        heads.reshape(2, -1),
        tails.reshape(2, -1),
        negatives.reshape(2, -1),
    )

    own = lax.all_to_all(returned.reshape(chips, 8, 384), "bucket", 0, 0, tiled=True).reshape(chips * 8, 384)

    half_sum = jax.ShapeDtypeStruct((16, 128), F32)
    half_spec = pl.BlockSpec((16, 128), lambda i, rep: (0, 0))
    keep, give = pl.pallas_call(
        relation_kernel,
        out_shape=(half_sum, half_sum),
        grid_spec=pltpu.PrefetchScalarGridSpec(
            num_scalar_prefetch=1,
            grid=(1,),
            in_specs=[pl.BlockSpec((chips * 8, 128), lambda i, rep: (0, 2))],
            out_specs=(half_spec, half_spec),
        ),
        compiler_params=limit(16),
        name="sum_relations",
    )(rep, own)
    sums = (keep + lax.ppermute(give, "rep", swap)).astype(BF16)
    gathered = gather_among(gather_among(sums, ALONG_Z), IN_PLANE)

    peer = lax.ppermute(own, "rep", swap)
    chunk = 256
    rows_spec = pl.BlockSpec((chips * 8, 256), lambda i: (0, 0))
    ids_spec = pl.BlockSpec((8, 256), lambda i: (0, 0))
    entity_grad = pl.pallas_call(
        scatter_kernel,
        out_shape=jax.ShapeDtypeStruct((entities, width), F32),
        grid=(entities // chunk,),
        in_specs=[rows_spec, rows_spec, ids_spec, ids_spec],
        out_specs=pl.BlockSpec((chunk, width), lambda i: (i, 0)),
        scratch_shapes=[pltpu.VMEM((1024, width), BF16)],
        compiler_params=limit(16),
        cost_estimate=pl.CostEstimate(flops=2 * 1024 * entities * width, bytes_accessed=16 << 20, transcendentals=0),
        name="scatter_rows",
    )(own, peer, ids, peer_ids)

    gathered, entity_grad = lax.optimization_barrier((gathered, entity_grad))
    peer_gathered = lax.ppermute(gathered, "rep", swap)
    relation_grad = pl.pallas_call(
        assemble_kernel,
        out_shape=jax.ShapeDtypeStruct(relations.shape, F32),
        grid_spec=pltpu.PrefetchScalarGridSpec(
            num_scalar_prefetch=1,
            grid=(1,),
            in_specs=[pl.BlockSpec((chips * 16, 128), lambda i, rep: (0, 0))] * 2,
            out_specs=pl.BlockSpec(relations.shape, lambda i, rep: (0, 0, 0, 0)),
        ),
        compiler_params=limit(24),
        name="assemble_relations",
    )(rep, gathered, peer_gathered)
    return entity_grad, relation_grad


def solution(mesh):
    return jax.shard_map(
        body,
        mesh=mesh,
        in_specs=(
            P("bucket", None),
            P(),
            P("bucket", "rep", None, None),
            P("bucket", "rep", None, None),
            P("bucket", "rep", None, None, None),
            P("bucket", "rep", None, None, None),
            P("bucket", "rep", None, None, None),
            P("bucket", "rep", None, None),
        ),
        out_specs=(P("bucket", None), P()),
        check_vma=False,
    )
```

```python
import functools

import jax
import jax.numpy as jnp
from jax import lax
from jax.experimental import pallas as pl
from jax.experimental.pallas import tpu as pltpu
from jax.sharding import PartitionSpec as P

F32 = jnp.float32
BF16 = jnp.bfloat16
VMEM = pl.BlockSpec(memory_space=pltpu.VMEM)
HBM = pl.BlockSpec(memory_space=pltpu.HBM)


def iota(shape, dim):
    return lax.broadcasted_iota(jnp.int32, shape, dim)


def dot(a, b, ca=1, cb=0):
    return lax.dot_general(a, b, (((ca,), (cb,)), ((), ())), preferred_element_type=F32)


def onehot(mask):
    return jnp.where(mask, 1.0, 0.0).astype(BF16)


def unpack_matrix():
    g = iota((256, 256), 0)
    p = iota((256, 256), 1)
    return onehot(p == (g & 31) * 8 + (g >> 5))


def pack_matrix():
    p = iota((256, 256), 0)
    g = iota((256, 256), 1)
    return onehot(p == (g & 31) * 8 + (g >> 5))


def slot_row(ids):
    return ((ids >> 6) << 6) | ((ids & 1) << 5) | ((ids >> 1) & 31)


def pack_slots(read, write):
    matrix = pack_matrix()
    for b in range(4):
        rows = jnp.concatenate(
            [read(k, b)[:, h * 256 : h * 256 + 256] for h in range(2) for k in range(2)], axis=0
        )
        write(b, dot(matrix, rows).astype(BF16))


def unpack_slots(read, write):
    matrix = unpack_matrix()
    for b in range(4):
        rows = dot(matrix, read(b)).astype(BF16)
        for h in range(2):
            for k in range(2):
                start = h * 128 + k * 64
                write(k, b, h, rows[start : start + 64])


def send_kernel(
    rows_hbm, count_hbm, table_ref, packed_ref, ids_ref, rows_ref, count_ref, table, slots, packed, list_sem, in_sem, out_sem
):
    part = table.shape[0] // 4
    lists = [
        pltpu.make_async_copy(rows_hbm, rows_ref, list_sem.at[0]),
        pltpu.make_async_copy(count_hbm, count_ref, list_sem.at[1]),
    ]
    for copy in lists:
        copy.start()

    def fetch(n):
        rows = pl.ds(n * part, part)
        return pltpu.make_async_copy(table_ref.at[rows], table.at[rows], in_sem.at[n])

    def send(b):
        rows = pl.ds(b * 256, 256)
        return pltpu.make_async_copy(packed.at[rows], packed_ref.at[rows], out_sem.at[b])

    for n in range(4):
        fetch(n).start()
    row = iota((256, 128), 0)
    dest = (row >> 6) * 32 + (row & 31)
    other = iota((256, 128), 1)
    column = (iota((256, 1), 0) >> 5) & 1
    flat = iota((256, 256), 1)
    entity = iota((256, part), 1)
    ids_ref[...] = jnp.zeros_like(ids_ref)
    wanted = []
    for copy in lists:
        copy.wait()
    for k in range(2):
        counts = count_ref[k : k + 1, :].astype(F32)
        start = jnp.sum(jnp.where(other < dest, counts, 0.0), axis=1, keepdims=True)
        count = jnp.sum(jnp.where(other == dest, counts, 0.0), axis=1, keepdims=True)
        position = start.astype(jnp.int32) + column
        names = rows_ref[k : k + 1, :].astype(F32)
        ids = jnp.sum(jnp.where(flat == position, names, 0.0), axis=1, keepdims=True)
        ids = jnp.where(column < count.astype(jnp.int32), ids, -1.0)
        ids_ref[k : k + 1, :] = jnp.transpose(jnp.broadcast_to(ids, (256, 128)))[0:1, :]
        wanted.append(ids.astype(jnp.int32))
    totals = [jnp.zeros(slots.shape[1:], F32) for k in range(2)]
    for n in range(4):
        fetch(n).wait()
        rows = table[n * part : n * part + part, :]
        for k in range(2):
            totals[k] = totals[k] + dot(onehot(entity + n * part == wanted[k]), rows)
    for k in range(2):
        slots[k] = totals[k].astype(BF16)

    def write(b, rows):
        packed[b * 256 : b * 256 + 256, :] = rows
        send(b).start()

    pack_slots(lambda k, b: slots[k, b * 64 : b * 64 + 64, :], write)
    for b in range(4):
        send(b).wait()


def count_kernel(rel_ref, first_ref, second_ref, heads_ref, tails_ref, neg_ref, names_ref, diag_ref, edges_ref, pairs_ref):
    neg_count = neg_ref.shape[1]
    names_ref[...] = jnp.where(iota((8, 128), 0) == 0, rel_ref[0], rel_ref[1]).astype(F32)
    for k in range(2):
        relation = (first_ref, second_ref)[k]
        for c in range(2):
            for j in range(4):
                place = onehot(iota((64, 256), 1) == iota((64, 256), 0) + 64 * j)
                diag_ref[k, c, 64 * j : 64 * j + 64, :] = dot(relation[0, 4 * c + j], place).astype(BF16)
        slot = iota((256, heads_ref.shape[1]), 0)
        at_head = onehot(slot == slot_row(heads_ref[k : k + 1, :]))
        at_tail = onehot(slot == slot_row(tails_ref[k : k + 1, :]))
        edges = dot(at_head, at_tail, 1, 1)
        head_edges = jnp.sum(edges, axis=1, keepdims=True)
        at_neg = onehot(iota((256, neg_count), 0) == slot_row(neg_ref[k : k + 1, :]))
        times = dot(jnp.ones((8, neg_count), BF16), at_neg, 1, 1)[0:1, :]
        edges_ref[k] = edges
        pairs_ref[k] = head_edges * times


def step_kernel(
    neg_count, packed_ref, names, diag, edges, pairs, out_ref, slots, grads, partial
):
    def write(k, b, h, rows):
        slots[k, b * 64 : b * 64 + 64, h * 256 : h * 256 + 256] = rows

    unpack_slots(lambda b: packed_ref[b * 256 : b * 256 + 256, :], write)
    lane_block = iota((64, 256), 1) >> 6
    for k in range(2):
        rows = slots[k]
        rotated = jnp.concatenate(
            [dot(rows[:, c * 256 : c * 256 + 256], diag[k, c]) for c in range(2)], axis=1
        ).astype(BF16)
        score = dot(rotated, rows, 1, 1)
        small = jnp.exp(-jnp.abs(score))
        big_side = 1.0 / (1.0 + small)
        small_side = small * big_side
        sigmoid = jnp.where(score >= 0, big_side, small_side)
        sigmoid_neg = jnp.where(score >= 0, small_side, big_side)
        weight = (pairs[k] * sigmoid / neg_count - edges[k] * sigmoid_neg).astype(BF16)
        grad_rotated = dot(weight, rows).astype(BF16)
        grad_other = dot(weight, rotated, 0, 0)
        for c in range(2):
            lanes = slice(c * 256, c * 256 + 256)
            grad_head = dot(grad_rotated[:, lanes], diag[k, c], 1, 1)
            grads[k, :, lanes] = (grad_head + grad_other[:, lanes]).astype(BF16)
            outer = dot(rows[:, lanes], grad_rotated[:, lanes], 0, 0)
            total = jnp.zeros((64, 256), F32)
            for j in range(4):
                total = jnp.where(lane_block == j, outer[64 * j : 64 * j + 64, :], total)
            partial[k, :, lanes] = total.astype(BF16)

    p = iota((256, 128), 0)
    g = iota((256, 128), 1)
    piece = p & 3
    source = ((p >> 2) & 1) * 64 + (((p >> 3) & 1) * 2 + piece) * 16 + ((p >> 4) & 1) * 8 + (p >> 5)
    spread = onehot((g == source) & (piece < 2))
    named = jnp.where(((p >> 2) & 1) == 0, names[0:1, :], names[1:2, :])

    def write_packed(b, rows):
        out_ref[b * 256 : b * 256 + 256, 0:256] = rows
        rows = jnp.concatenate(
            [partial[k, b * 16 : b * 16 + 16, q * 128 : q * 128 + 128] for k in range(2) for q in range(4)], axis=0
        )
        out_ref[b * 256 : b * 256 + 256, 256:384] = jnp.where(piece == 2, named, dot(spread, rows)).astype(BF16)

    pack_slots(lambda k, b: grads[k, b * 64 : b * 64 + 64, :], write_packed)


def relation_kernel(rep_ref, own_ref, keep_ref, give_ref):
    matrix = unpack_matrix()
    lane = iota((128, 128), 1)
    totals = [jnp.zeros((128, 128), F32) for q in range(2)]
    blocks = [dot(matrix, own_ref[b * 256 : b * 256 + 256, :]) for b in range(4)]

    def piece(index):
        return jnp.concatenate([rows[index * 32 : index * 32 + 32] for rows in blocks], axis=0)

    for k in range(2):
        chosen = onehot(lane == piece(4 * k + 2).astype(jnp.int32))
        for q in range(2):
            totals[q] = totals[q] + dot(chosen, piece(4 * k + q).astype(BF16), 0, 0)
    first = rep_ref[0] == 0
    keep_ref[...] = jnp.where(first, totals[0], totals[1])[0:16]
    give_ref[...] = jnp.where(first, totals[1], totals[0])[0:16]


def scatter_kernel(own_ref, peer_ref, own_ids, peer_ids, out_ref, rows_ref):
    @pl.when(pl.program_id(0) == 0)
    def _():
        for r, ref in enumerate((own_ref, peer_ref)):

            def write(k, b, h, rows):
                start = (r * 2 + k) * 256 + b * 64
                rows_ref[start : start + 64, h * 256 : h * 256 + 256] = rows

            unpack_slots(lambda b: ref[b * 256 : b * 256 + 256, :], write)

    base = pl.program_id(0) * 256
    entity = iota((256, 256), 0) + base
    total = jnp.zeros(out_ref.shape, F32)
    for r, ref in enumerate((own_ids, peer_ids)):
        for k in range(2):
            start = (r * 2 + k) * 256
            hit = onehot(entity == ref[k : k + 1, :].astype(jnp.int32))
            total = total + dot(hit, rows_ref[start : start + 256, :])
    out_ref[...] = total


def assemble_kernel(place_ref, *refs):
    pieces, out_ref = refs[:4], refs[-1]
    g = iota((256, 256), 0)
    p = iota((256, 256), 1)
    matrix = onehot(p == (g & 15) * 16 + (g >> 4))
    for shift in range(4):

        @pl.when(pl.program_id(0) == shift)
        def _():
            for y in range(2):
                rows = dot(matrix, pieces[shift][y * 256 : y * 256 + 256, :]).reshape(16, 2, 8, 128)
                for side in range(2):
                    out_ref[:, 0, 0, side, 2 * y : 2 * y + 2, 0] = rows[:, :, :, 64 * side : 64 * side + 64]


def chip(y, z, x):
    return (y * 8 + z) * 4 + x


ACROSS_YZ = [[chip(y, z, x) for y in range(4) for z in range(8)] for x in range(4)]


def along_x(step):
    return [(chip(y, z, x), chip(y, z, (x + step) % 4)) for y in range(4) for z in range(8) for x in range(4)]


def gather_among(rows, groups):
    count = len(groups[0])
    spread = jnp.broadcast_to(rows[None], (count,) + rows.shape)
    out = lax.all_to_all(spread, "bucket", 0, 0, axis_index_groups=groups, tiled=True)
    return out.reshape(count * rows.shape[0], rows.shape[1])


def assemble(place, pieces, into):
    view = (16, 2, 2, 2, 4, 2, 8, 64)

    def where(shift, place):
        x = (place[0] - shift) & 3
        return (0, x & 1, place[1], 0, 0, x >> 1, 0, 0)

    arrays = list(pieces) + ([] if into is None else [into])
    specs = [pl.BlockSpec(pieces[0].shape, lambda shift, place: (0, 0))] * 4
    if into is not None:
        specs.append(pl.BlockSpec(memory_space=pl.ANY))
    return pl.pallas_call(
        assemble_kernel,
        out_shape=jax.ShapeDtypeStruct(view, F32),
        grid_spec=pltpu.PrefetchScalarGridSpec(
            num_scalar_prefetch=1,
            grid=(4,),
            in_specs=specs,
            out_specs=pl.BlockSpec((16, 1, 1, 2, 4, 1, 8, 64), where),
        ),
        input_output_aliases={} if into is None else {5: 0},
        compiler_params=limit(8),
        cost_estimate=pl.CostEstimate(flops=1 << 27, bytes_accessed=3 << 20, transcendentals=0),
        name="assemble_relations",
    )(place, *arrays)


def limit(mib):
    return pltpu.CompilerParams(vmem_limit_bytes=mib << 20)


def body(entity_table, relations, send_rows, send_count, heads, tails, negatives, span_rel):
    entities, width = entity_table.shape
    chips = send_count.shape[3]
    rep = lax.axis_index("rep").astype(jnp.int32).reshape(1)
    swap = [(0, 1), (1, 0)]

    packed, ids = pl.pallas_call(
        send_kernel,
        out_shape=(jax.ShapeDtypeStruct((chips * 8, 256), BF16), jax.ShapeDtypeStruct((8, 256), F32)),
        in_specs=[HBM, HBM, HBM],
        out_specs=(HBM, VMEM),
        scratch_shapes=[
            pltpu.VMEM(send_rows.shape[2:], jnp.int32),
            pltpu.VMEM(send_count.shape[2:], jnp.int32),
            pltpu.VMEM((entities, width), BF16),
            pltpu.VMEM((2, 256, width), BF16),
            pltpu.VMEM((chips * 8, 256), BF16),
            pltpu.SemaphoreType.DMA((2,)),
            pltpu.SemaphoreType.DMA((4,)),
            pltpu.SemaphoreType.DMA((4,)),
        ],
        name="send_rows",
    )(send_rows[0, 0], send_count[0, 0], entity_table)
    peer_ids = lax.ppermute(ids, "rep", swap)

    received = lax.all_to_all(packed.reshape(chips, 8, 256), "bucket", 0, 0, tiled=True).reshape(chips * 8, 256)
    rel_ids = span_rel.reshape(2)
    neg_count = negatives.shape[4]
    whole = lambda shape: pl.BlockSpec(shape, lambda i, rel: (0,) * len(shape))
    relation_spec = lambda k: pl.BlockSpec((1, 8, 64, 64), lambda i, rel: (rel[k], 0, 0, 0))
    shapes = ((8, 128), (2, 2, 256, 256), (2, 256, 256), (2, 256, 256))
    counts = pl.pallas_call(
        count_kernel,
        out_shape=tuple(jax.ShapeDtypeStruct(shape, t) for shape, t in zip(shapes, (F32, BF16, F32, F32))),
        grid_spec=pltpu.PrefetchScalarGridSpec(
            num_scalar_prefetch=1,
            grid=(1,),
            in_specs=[
                relation_spec(0),
                relation_spec(1),
                whole((2, heads.shape[4])),
                whole((2, tails.shape[4])),
                whole((2, neg_count)),
            ],
            out_specs=tuple(whole(shape) for shape in shapes),
        ),
        compiler_params=limit(16),
        cost_estimate=pl.CostEstimate(flops=1 << 28, bytes_accessed=4 << 20, transcendentals=0),
        name="count_edges",
    )(rel_ids, relations, relations, heads.reshape(2, -1), tails.reshape(2, -1), negatives.reshape(2, -1))

    received, peer_ids, *counts = lax.optimization_barrier((received, peer_ids, *counts))
    returned = pl.pallas_call(
        functools.partial(step_kernel, neg_count),
        out_shape=jax.ShapeDtypeStruct((chips * 8, 384), BF16),
        in_specs=[VMEM] * 5,
        out_specs=VMEM,
        scratch_shapes=[
            pltpu.VMEM((2, 256, width), BF16),
            pltpu.VMEM((2, 256, width), BF16),
            pltpu.VMEM((2, 64, width), BF16),
        ],
        compiler_params=limit(24),
        name="train_step",
    )(received, *counts)

    own = lax.all_to_all(returned.reshape(chips, 8, 384), "bucket", 0, 0, tiled=True).reshape(chips * 8, 384)

    half_sum = jax.ShapeDtypeStruct((16, 128), F32)
    half_spec = pl.BlockSpec((16, 128), lambda i, rep: (0, 0))
    keep, give = pl.pallas_call(
        relation_kernel,
        out_shape=(half_sum, half_sum),
        grid_spec=pltpu.PrefetchScalarGridSpec(
            num_scalar_prefetch=1,
            grid=(1,),
            in_specs=[pl.BlockSpec((chips * 8, 128), lambda i, rep: (0, 2))],
            out_specs=(half_spec, half_spec),
        ),
        compiler_params=limit(16),
        name="sum_relations",
    )(rep, own)
    sums = (keep + lax.ppermute(give, "rep", swap)).astype(BF16)
    column = gather_among(sums, ACROSS_YZ)
    pieces = [column] + [lax.ppermute(column, "bucket", along_x(step)) for step in (1, 2, 3)]

    peer = lax.ppermute(own, "rep", swap)
    chunk = 256
    rows_spec = pl.BlockSpec((chips * 8, 256), lambda i: (0, 0))
    ids_spec = pl.BlockSpec((8, 256), lambda i: (0, 0))
    entity_grad = pl.pallas_call(
        scatter_kernel,
        out_shape=jax.ShapeDtypeStruct((entities, width), F32),
        grid=(entities // chunk,),
        in_specs=[rows_spec, rows_spec, ids_spec, ids_spec],
        out_specs=pl.BlockSpec((chunk, width), lambda i: (i, 0)),
        scratch_shapes=[pltpu.VMEM((1024, width), BF16)],
        compiler_params=limit(16),
        cost_estimate=pl.CostEstimate(flops=2 * 1024 * entities * width, bytes_accessed=16 << 20, transcendentals=0),
        name="scatter_rows",
    )(own, peer, ids, peer_ids)

    *pieces, entity_grad = lax.optimization_barrier((*pieces, entity_grad))
    peer_pieces = [lax.ppermute(piece, "rep", swap) for piece in pieces]
    x = lax.axis_index("bucket").astype(jnp.int32).reshape(1) & 3
    relation_grad = assemble(jnp.concatenate([x, rep]), pieces, None)
    relation_grad = assemble(jnp.concatenate([x, 1 - rep]), peer_pieces, relation_grad)
    relation_grad = relation_grad.reshape(relations.shape)
    return entity_grad, relation_grad


def solution(mesh):
    return jax.shard_map(
        body,
        mesh=mesh,
        in_specs=(
            P("bucket", None),
            P(),
            P("bucket", "rep", None, None),
            P("bucket", "rep", None, None),
            P("bucket", "rep", None, None, None),
            P("bucket", "rep", None, None, None),
            P("bucket", "rep", None, None, None),
            P("bucket", "rep", None, None),
        ),
        out_specs=(P("bucket", None), P()),
        check_vma=False,
    )
```

```python
import functools

import jax
import jax.numpy as jnp
from jax import lax
from jax.experimental import pallas as pl
from jax.experimental.pallas import tpu as pltpu
from jax.sharding import PartitionSpec as P

F32 = jnp.float32
BF16 = jnp.bfloat16
VMEM = pl.BlockSpec(memory_space=pltpu.VMEM)
HBM = pl.BlockSpec(memory_space=pltpu.HBM)


def iota(shape, dim):
    return lax.broadcasted_iota(jnp.int32, shape, dim)


def dot(a, b, ca=1, cb=0):
    return lax.dot_general(a, b, (((ca,), (cb,)), ((), ())), preferred_element_type=F32)


def onehot(mask):
    return jnp.where(mask, 1.0, 0.0).astype(BF16)


def unpack_matrix():
    g = iota((256, 256), 0)
    p = iota((256, 256), 1)
    return onehot(p == (g & 31) * 8 + (g >> 5))


def pack_matrix():
    p = iota((256, 256), 0)
    g = iota((256, 256), 1)
    return onehot(p == (g & 31) * 8 + (g >> 5))


def slot_row(ids):
    return ((ids >> 6) << 6) | ((ids & 1) << 5) | ((ids >> 1) & 31)


def pack_slots(read, write):
    matrix = pack_matrix()
    for b in range(4):
        rows = jnp.concatenate(
            [read(k, b)[:, h * 256 : h * 256 + 256] for h in range(2) for k in range(2)], axis=0
        )
        write(b, dot(matrix, rows).astype(BF16))


def unpack_slots(read, write):
    matrix = unpack_matrix()
    for b in range(4):
        rows = dot(matrix, read(b)).astype(BF16)
        for h in range(2):
            for k in range(2):
                start = h * 128 + k * 64
                write(k, b, h, rows[start : start + 64])


def send_kernel(
    rows_hbm, count_hbm, table_ref, packed_ref, ids_ref, rows_ref, count_ref, table, slots, packed, list_sem, in_sem, out_sem
):
    part = table.shape[0] // 4
    lists = [
        pltpu.make_async_copy(rows_hbm, rows_ref, list_sem.at[0]),
        pltpu.make_async_copy(count_hbm, count_ref, list_sem.at[1]),
    ]
    for copy in lists:
        copy.start()

    def fetch(n):
        rows = pl.ds(n * part, part)
        return pltpu.make_async_copy(table_ref.at[rows], table.at[rows], in_sem.at[n])

    def send(b):
        rows = pl.ds(b * 256, 256)
        return pltpu.make_async_copy(packed.at[rows], packed_ref.at[rows], out_sem.at[b])

    for n in range(4):
        fetch(n).start()
    row = iota((512, 128), 0) & 255
    dest = (row >> 6) * 32 + (row & 31)
    other = iota((512, 128), 1)
    column = (iota((512, 1), 0) >> 5) & 1
    for copy in lists:
        copy.wait()

    def both(ref):
        values = ref[...].astype(F32)
        return jnp.concatenate(
            [jnp.broadcast_to(values[k : k + 1], (256, values.shape[1])) for k in range(2)], axis=0
        )

    counts = both(count_ref)
    start = jnp.sum(jnp.where(other < dest, counts, 0.0), axis=1, keepdims=True)
    count = jnp.sum(jnp.where(other == dest, counts, 0.0), axis=1, keepdims=True)
    position = start.astype(jnp.int32) + column
    ids = jnp.sum(jnp.where(iota((512, 256), 1) == position, both(rows_ref), 0.0), axis=1, keepdims=True)
    ids = jnp.where(column < count.astype(jnp.int32), ids, -1.0)
    wanted = ids.astype(jnp.int32)
    entity = iota((512, part), 1)
    total = jnp.zeros((512, table.shape[1]), F32)
    for n in range(4):
        fetch(n).wait()
        total = total + dot(onehot(entity + n * part == wanted), table[n * part : n * part + part, :])
    slots[...] = total.astype(BF16)
    ids_ref[...] = jnp.zeros_like(ids_ref)
    for k in range(2):
        spread = jnp.broadcast_to(ids[k * 256 : k * 256 + 256], (256, 128))
        ids_ref[k : k + 1, :] = jnp.transpose(spread)[0:1, :]

    def write(b, rows):
        packed[b * 256 : b * 256 + 256, :] = rows
        send(b).start()

    pack_slots(lambda k, b: slots[k * 256 + b * 64 : k * 256 + b * 64 + 64, :], write)
    for b in range(4):
        send(b).wait()


def count_kernel(rel_ref, relation_ref, heads_ref, tails_ref, neg_ref, names_ref, diag_ref, edges_ref, times_ref):
    neg_count = neg_ref.shape[1]
    names_ref[...] = jnp.where(iota((8, 128), 0) == 0, rel_ref[0], rel_ref[1]).astype(F32)
    for k in range(2):
        for c in range(2):
            for j in range(4):
                place = onehot(iota((64, 256), 1) == iota((64, 256), 0) + 64 * j)
                diag_ref[k, c, 64 * j : 64 * j + 64, :] = dot(relation_ref[k, 4 * c + j], place).astype(BF16)
        slot = iota((256, heads_ref.shape[1]), 0)
        at_head = onehot(slot == slot_row(heads_ref[k : k + 1, :]))
        at_tail = onehot(slot == slot_row(tails_ref[k : k + 1, :]))
        edges = dot(at_head, at_tail, 1, 1)
        at_neg = onehot(iota((256, neg_count), 0) == slot_row(neg_ref[k : k + 1, :]))
        edges_ref[k] = edges
        times_ref[k] = dot(jnp.ones((8, neg_count), BF16), at_neg, 1, 1)


def step_kernel(
    neg_count, packed_ref, names, diag, edges, times, out_ref, slots, grads, partial
):
    def write(k, b, h, rows):
        slots[k, b * 64 : b * 64 + 64, h * 256 : h * 256 + 256] = rows

    unpack_slots(lambda b: packed_ref[b * 256 : b * 256 + 256, :], write)
    lane_block = iota((64, 256), 1) >> 6
    for k in range(2):
        rows = slots[k]
        rotated = jnp.concatenate(
            [dot(rows[:, c * 256 : c * 256 + 256], diag[k, c]) for c in range(2)], axis=1
        ).astype(BF16)
        score = dot(rotated, rows, 1, 1)
        small = jnp.exp(-jnp.abs(score))
        big_side = 1.0 / (1.0 + small)
        small_side = small * big_side
        sigmoid = jnp.where(score >= 0, big_side, small_side)
        sigmoid_neg = jnp.where(score >= 0, small_side, big_side)
        pairs = jnp.sum(edges[k], axis=1, keepdims=True) * times[k][0:1, :]
        weight = (pairs * sigmoid / neg_count - edges[k] * sigmoid_neg).astype(BF16)
        grad_rotated = dot(weight, rows).astype(BF16)
        grad_other = dot(weight, rotated, 0, 0)
        for c in range(2):
            lanes = slice(c * 256, c * 256 + 256)
            grad_head = dot(grad_rotated[:, lanes], diag[k, c], 1, 1)
            grads[k, :, lanes] = (grad_head + grad_other[:, lanes]).astype(BF16)
            outer = dot(rows[:, lanes], grad_rotated[:, lanes], 0, 0)
            total = jnp.zeros((64, 256), F32)
            for j in range(4):
                total = jnp.where(lane_block == j, outer[64 * j : 64 * j + 64, :], total)
            partial[k, :, lanes] = total

    p = iota((256, 128), 0)
    g = iota((256, 128), 1)
    piece = p & 3
    source = ((p >> 2) & 1) * 64 + piece * 32 + ((p >> 3) & 3) * 8 + (p >> 5)
    spread = onehot((g == source) & (piece < 2))
    named = jnp.where(((p >> 2) & 1) == 0, names[0:1, :], names[1:2, :])

    def write_packed(b, rows):
        out_ref[b * 256 : b * 256 + 256, 0:256] = rows
        rows = jnp.concatenate(
            [
                partial[k, q * 32 + b * 8 : q * 32 + b * 8 + 8, x * 128 : x * 128 + 128]
                for k in range(2)
                for q in range(2)
                for x in range(4)
            ],
            axis=0,
        ).astype(BF16)
        out_ref[b * 256 : b * 256 + 256, 256:384] = jnp.where(piece == 2, named, dot(spread, rows)).astype(BF16)

    pack_slots(lambda k, b: grads[k, b * 64 : b * 64 + 64, :], write_packed)


def relation_kernel(rep_ref, own_ref, keep_ref, give_ref):
    matrix = unpack_matrix()
    lane = iota((128, 128), 1)
    totals = [jnp.zeros((128, 128), F32) for q in range(2)]
    blocks = [dot(matrix, own_ref[b * 256 : b * 256 + 256, :]) for b in range(4)]

    def piece(index):
        return jnp.concatenate([rows[index * 32 : index * 32 + 32] for rows in blocks], axis=0)

    for k in range(2):
        chosen = onehot(lane == piece(4 * k + 2).astype(jnp.int32))
        for q in range(2):
            totals[q] = totals[q] + dot(chosen, piece(4 * k + q).astype(BF16), 0, 0)
    first = rep_ref[0] == 0
    keep_ref[...] = jnp.where(first, totals[0], totals[1])[0:16]
    give_ref[...] = jnp.where(first, totals[1], totals[0])[0:16]


def scatter_kernel(own_ref, peer_ref, own_ids, peer_ids, out_ref, rows_ref):
    @pl.when(pl.program_id(0) == 0)
    def _():
        for r, ref in enumerate((own_ref, peer_ref)):

            def write(k, b, h, rows):
                start = (r * 2 + k) * 256 + b * 64
                rows_ref[start : start + 64, h * 256 : h * 256 + 256] = rows

            unpack_slots(lambda b: ref[b * 256 : b * 256 + 256, :], write)

    base = pl.program_id(0) * 256
    entity = iota((256, 256), 0) + base
    total = jnp.zeros(out_ref.shape, F32)
    for r, ref in enumerate((own_ids, peer_ids)):
        for k in range(2):
            start = (r * 2 + k) * 256
            hit = onehot(entity == ref[k : k + 1, :].astype(jnp.int32))
            total = total + dot(hit, rows_ref[start : start + 256, :])
    out_ref[...] = total


def order_kernel(rows_ref, out_ref):
    g = iota((256, 256), 0)
    p = iota((256, 256), 1)
    matrix = onehot(p == (g & 15) * 16 + (g >> 4))
    for y in range(2):
        out_ref[y * 256 : y * 256 + 256, :] = dot(matrix, rows_ref[y * 256 : y * 256 + 256, :]).astype(BF16)


def widen(piece, result):
    for y in range(2):
        rows = piece[y * 256 : y * 256 + 256, :].astype(F32).reshape(16, 16, 128)
        for side in range(2):
            result[:, side, y * 16 : y * 16 + 16] = rows[:, :, 64 * side : 64 * side + 64]


def widen_kernel(*refs):
    for n, piece in enumerate(refs[:-1]):
        widen(piece, refs[-1].at[n])


def lay_out_kernel(count, ready, xs_ref, qs_ref, *refs):
    pieces = refs[:count]
    out_ref, result, sem = refs[-3:]
    copies = []

    def send(n, source):
        copy = pltpu.make_async_copy(source, out_ref.at[:, xs_ref[n], :, qs_ref[n]], sem.at[n])
        copy.start()
        copies.append(copy)

    for n in range(ready):
        send(count + n, refs[count].at[n])
    for n in range(count):
        widen(pieces[n], result.at[n])
        send(n, result.at[n])
    for copy in copies:
        copy.wait()


def chip(y, z, x):
    return (y * 8 + z) * 4 + x


ACROSS_YZ = [[chip(y, z, x) for y in range(4) for z in range(8)] for x in range(4)]


def along_x(step):
    return [(chip(y, z, x), chip(y, z, (x + step) % 4)) for y in range(4) for z in range(8) for x in range(4)]


def gather_among(rows, groups):
    count = len(groups[0])
    spread = jnp.broadcast_to(rows[None], (count,) + rows.shape)
    out = lax.all_to_all(spread, "bucket", 0, 0, axis_index_groups=groups, tiled=True)
    return out.reshape(count * rows.shape[0], rows.shape[1])


WIDE = (16, 2, 32, 64)


def lay_out(pieces, wide, xs, qs, into):
    view = (16, 4, 2, 2, 32, 64)
    count = len(pieces)
    ready = 0 if wide is None else wide.shape[0]
    arrays = list(pieces) + ([] if wide is None else [wide])
    earlier = [] if into is None else [into]
    scalars = pl.BlockSpec(memory_space=pltpu.SMEM)
    return pl.pallas_call(
        functools.partial(lay_out_kernel, count, ready),
        out_shape=jax.ShapeDtypeStruct(view, F32),
        in_specs=[scalars] * 2 + [VMEM] * len(arrays) + [HBM] * len(earlier),
        out_specs=HBM,
        scratch_shapes=[pltpu.VMEM((count,) + WIDE, F32), pltpu.SemaphoreType.DMA((count + ready,))],
        input_output_aliases={2 + len(arrays): 0} if earlier else {},
        compiler_params=limit(8),
        cost_estimate=pl.CostEstimate(flops=1 << 20, bytes_accessed=count << 20, transcendentals=0),
        name="lay_out_relations",
    )(xs, qs, *arrays, *earlier)


def limit(mib):
    return pltpu.CompilerParams(vmem_limit_bytes=mib << 20)


def body(entity_table, relations, send_rows, send_count, heads, tails, negatives, span_rel):
    entities, width = entity_table.shape
    chips = send_count.shape[3]
    rep = lax.axis_index("rep").astype(jnp.int32).reshape(1)
    swap = [(0, 1), (1, 0)]

    packed, ids = pl.pallas_call(
        send_kernel,
        out_shape=(jax.ShapeDtypeStruct((chips * 8, 256), BF16), jax.ShapeDtypeStruct((8, 256), F32)),
        in_specs=[HBM, HBM, HBM],
        out_specs=(HBM, VMEM),
        scratch_shapes=[
            pltpu.VMEM(send_rows.shape[2:], jnp.int32),
            pltpu.VMEM(send_count.shape[2:], jnp.int32),
            pltpu.VMEM((entities, width), BF16),
            pltpu.VMEM((512, width), BF16),
            pltpu.VMEM((chips * 8, 256), BF16),
            pltpu.SemaphoreType.DMA((2,)),
            pltpu.SemaphoreType.DMA((4,)),
            pltpu.SemaphoreType.DMA((4,)),
        ],
        name="send_rows",
    )(send_rows[0, 0], send_count[0, 0], entity_table)
    peer_ids = lax.ppermute(ids, "rep", swap)

    received = lax.all_to_all(packed.reshape(chips, 8, 256), "bucket", 0, 0, tiled=True).reshape(chips * 8, 256)
    rel_ids = span_rel.reshape(2)
    neg_count = negatives.shape[4]
    used = jnp.concatenate([lax.dynamic_slice_in_dim(relations, rel_ids[k], 1) for k in range(2)])
    shapes = ((8, 128), (2, 2, 256, 256), (2, 256, 256), (2, 8, 256))
    counts = pl.pallas_call(
        count_kernel,
        out_shape=tuple(jax.ShapeDtypeStruct(shape, t) for shape, t in zip(shapes, (F32, BF16, F32, F32))),
        in_specs=[pl.BlockSpec(memory_space=pltpu.SMEM)] + [VMEM] * 4,
        out_specs=(VMEM,) * 4,
        compiler_params=limit(16),
        cost_estimate=pl.CostEstimate(flops=1 << 28, bytes_accessed=4 << 20, transcendentals=0),
        name="count_edges",
    )(rel_ids, used, heads.reshape(2, -1), tails.reshape(2, -1), negatives.reshape(2, -1))

    received, peer_ids, *counts = lax.optimization_barrier((received, peer_ids, *counts))
    returned = pl.pallas_call(
        functools.partial(step_kernel, neg_count),
        out_shape=jax.ShapeDtypeStruct((chips * 8, 384), BF16),
        in_specs=[VMEM] * 5,
        out_specs=VMEM,
        scratch_shapes=[
            pltpu.VMEM((2, 256, width), BF16),
            pltpu.VMEM((2, 256, width), BF16),
            pltpu.VMEM((2, 64, width), F32),
        ],
        compiler_params=limit(24),
        name="train_step",
    )(received, *counts)

    own = lax.all_to_all(returned.reshape(chips, 8, 384), "bucket", 0, 0, tiled=True).reshape(chips * 8, 384)

    half_sum = jax.ShapeDtypeStruct((16, 128), F32)
    half_spec = pl.BlockSpec((16, 128), lambda i, rep: (0, 0))
    keep, give = pl.pallas_call(
        relation_kernel,
        out_shape=(half_sum, half_sum),
        grid_spec=pltpu.PrefetchScalarGridSpec(
            num_scalar_prefetch=1,
            grid=(1,),
            in_specs=[pl.BlockSpec((chips * 8, 128), lambda i, rep: (0, 2))],
            out_specs=(half_spec, half_spec),
        ),
        compiler_params=limit(16),
        name="sum_relations",
    )(rep, own)
    sums = (keep + lax.ppermute(give, "rep", swap)).astype(BF16)
    column = gather_among(sums, ACROSS_YZ)
    peer = lax.ppermute(own, "rep", swap)
    chunk = 256
    rows_spec = pl.BlockSpec((chips * 8, 256), lambda i: (0, 0))
    ids_spec = pl.BlockSpec((8, 256), lambda i: (0, 0))
    entity_grad = pl.pallas_call(
        scatter_kernel,
        out_shape=jax.ShapeDtypeStruct((entities, width), F32),
        grid=(entities // chunk,),
        in_specs=[rows_spec, rows_spec, ids_spec, ids_spec],
        out_specs=pl.BlockSpec((chunk, width), lambda i: (i, 0)),
        scratch_shapes=[pltpu.VMEM((1024, width), BF16)],
        compiler_params=limit(16),
        cost_estimate=pl.CostEstimate(flops=2 * 1024 * entities * width, bytes_accessed=16 << 20, transcendentals=0),
        name="scatter_rows",
    )(own, peer, ids, peer_ids)

    column, entity_grad = lax.optimization_barrier((column, entity_grad))
    column = pl.pallas_call(
        order_kernel,
        out_shape=jax.ShapeDtypeStruct(column.shape, BF16),
        in_specs=[VMEM],
        out_specs=VMEM,
        compiler_params=limit(8),
        name="order_column",
    )(column)
    pieces = [column] + [lax.ppermute(column, "bucket", along_x(step)) for step in (1, 2, 3)]

    x = lax.axis_index("bucket").astype(jnp.int32) & 3
    xs = (x - jnp.arange(4, dtype=jnp.int32)) & 3
    own_q = jnp.broadcast_to(rep, (4,))
    relation_grad = lay_out(pieces[:1], None, xs[:1], own_q[:1], None)
    peer_pieces = []
    for n in range(4):
        pieces[n], relation_grad = lax.optimization_barrier((pieces[n], relation_grad))
        peer_pieces.append(lax.ppermute(pieces[n], "rep", swap))
    wide = pl.pallas_call(
        widen_kernel,
        out_shape=jax.ShapeDtypeStruct((3,) + WIDE, F32),
        in_specs=[VMEM] * 3,
        out_specs=VMEM,
        compiler_params=limit(8),
        cost_estimate=pl.CostEstimate(flops=1 << 20, bytes_accessed=3 << 20, transcendentals=0),
        name="widen_own",
    )(*pieces[1:])
    relation_grad = lay_out(
        peer_pieces, wide, jnp.concatenate([xs, xs[1:]]), jnp.concatenate([1 - own_q, own_q[1:]]), relation_grad
    )
    relation_grad = relation_grad.reshape(relations.shape)
    return entity_grad, relation_grad


def solution(mesh):
    return jax.shard_map(
        body,
        mesh=mesh,
        in_specs=(
            P("bucket", None),
            P(),
            P("bucket", "rep", None, None),
            P("bucket", "rep", None, None),
            P("bucket", "rep", None, None, None),
            P("bucket", "rep", None, None, None),
            P("bucket", "rep", None, None, None),
            P("bucket", "rep", None, None),
        ),
        out_specs=(P("bucket", None), P()),
        check_vma=False,
    )
```

```python
import functools

import jax
import jax.numpy as jnp
from jax import lax
from jax.experimental import pallas as pl
from jax.experimental.pallas import tpu as pltpu
from jax.sharding import PartitionSpec as P

F32 = jnp.float32
BF16 = jnp.bfloat16
VMEM = pl.BlockSpec(memory_space=pltpu.VMEM)
HBM = pl.BlockSpec(memory_space=pltpu.HBM)


def iota(shape, dim):
    return lax.broadcasted_iota(jnp.int32, shape, dim)


def dot(a, b, ca=1, cb=0):
    return lax.dot_general(a, b, (((ca,), (cb,)), ((), ())), preferred_element_type=F32)


def onehot(mask):
    return jnp.where(mask, 1.0, 0.0).astype(BF16)


def unpack_matrix():
    g = iota((256, 256), 0)
    p = iota((256, 256), 1)
    return onehot(p == (g & 31) * 8 + (g >> 5))


def pack_matrix():
    p = iota((256, 256), 0)
    g = iota((256, 256), 1)
    return onehot(p == (g & 31) * 8 + (g >> 5))


def slot_row(ids):
    return ((ids >> 6) << 6) | ((ids & 1) << 5) | ((ids >> 1) & 31)


def pack_slots(read, write):
    matrix = pack_matrix()
    for b in range(4):
        rows = jnp.concatenate(
            [read(k, b)[:, h * 256 : h * 256 + 256] for h in range(2) for k in range(2)], axis=0
        )
        write(b, dot(matrix, rows).astype(BF16))


def unpack_slots(read, write):
    matrix = unpack_matrix()
    for b in range(4):
        rows = dot(matrix, read(b)).astype(BF16)
        for h in range(2):
            for k in range(2):
                start = h * 128 + k * 64
                write(k, b, h, rows[start : start + 64])


def send_kernel(
    rows_hbm, count_hbm, table_ref, packed_ref, ids_ref, rows_ref, count_ref, table, slots, packed, list_sem, in_sem, out_sem
):
    part = table.shape[0] // 4
    lists = [
        pltpu.make_async_copy(rows_hbm, rows_ref, list_sem.at[0]),
        pltpu.make_async_copy(count_hbm, count_ref, list_sem.at[1]),
    ]
    for copy in lists:
        copy.start()

    def fetch(n):
        rows = pl.ds(n * part, part)
        return pltpu.make_async_copy(table_ref.at[rows], table.at[rows], in_sem.at[n])

    def send(b):
        rows = pl.ds(b * 256, 256)
        return pltpu.make_async_copy(packed.at[rows], packed_ref.at[rows], out_sem.at[b])

    for n in range(4):
        fetch(n).start()
    row = iota((512, 128), 0) & 255
    dest = (row >> 6) * 32 + (row & 31)
    other = iota((512, 128), 1)
    column = (iota((512, 1), 0) >> 5) & 1
    for copy in lists:
        copy.wait()

    def both(ref):
        values = ref[...].astype(F32)
        return jnp.concatenate(
            [jnp.broadcast_to(values[k : k + 1], (256, values.shape[1])) for k in range(2)], axis=0
        )

    counts = both(count_ref)
    start = jnp.sum(jnp.where(other < dest, counts, 0.0), axis=1, keepdims=True)
    count = jnp.sum(jnp.where(other == dest, counts, 0.0), axis=1, keepdims=True)
    position = start.astype(jnp.int32) + column
    ids = jnp.sum(jnp.where(iota((512, 256), 1) == position, both(rows_ref), 0.0), axis=1, keepdims=True)
    ids = jnp.where(column < count.astype(jnp.int32), ids, -1.0)
    wanted = ids.astype(jnp.int32)
    entity = iota((512, part), 1)
    total = jnp.zeros((512, table.shape[1]), F32)
    for n in range(4):
        fetch(n).wait()
        total = total + dot(onehot(entity + n * part == wanted), table[n * part : n * part + part, :])
    slots[...] = total.astype(BF16)
    ids_ref[...] = jnp.zeros_like(ids_ref)
    for k in range(2):
        spread = jnp.broadcast_to(ids[k * 256 : k * 256 + 256], (256, 128))
        ids_ref[k : k + 1, :] = jnp.transpose(spread)[0:1, :]

    def write(b, rows):
        packed[b * 256 : b * 256 + 256, :] = rows
        send(b).start()

    pack_slots(lambda k, b: slots[k * 256 + b * 64 : k * 256 + b * 64 + 64, :], write)
    for b in range(4):
        send(b).wait()


def count_kernel(rel_ref, relation_ref, heads_ref, tails_ref, neg_ref, names_ref, diag_ref, edges_ref, times_ref):
    neg_count = neg_ref.shape[1]
    names_ref[...] = jnp.where(iota((8, 128), 0) == 0, rel_ref[0], rel_ref[1]).astype(F32)
    for k in range(2):
        for c in range(2):
            for j in range(4):
                place = onehot(iota((64, 256), 1) == iota((64, 256), 0) + 64 * j)
                diag_ref[k, c, 64 * j : 64 * j + 64, :] = dot(relation_ref[k, 4 * c + j], place).astype(BF16)
        slot = iota((256, heads_ref.shape[1]), 0)
        at_head = onehot(slot == slot_row(heads_ref[k : k + 1, :]))
        at_tail = onehot(slot == slot_row(tails_ref[k : k + 1, :]))
        edges = dot(at_head, at_tail, 1, 1)
        at_neg = onehot(iota((256, neg_count), 0) == slot_row(neg_ref[k : k + 1, :]))
        edges_ref[k] = edges
        times_ref[k] = dot(jnp.ones((8, neg_count), BF16), at_neg, 1, 1)


def step_kernel(
    neg_count, packed_ref, names, diag, edges, times, out_ref, slots, grads, partial
):
    def write(k, b, h, rows):
        slots[k, b * 64 : b * 64 + 64, h * 256 : h * 256 + 256] = rows

    unpack_slots(lambda b: packed_ref[b * 256 : b * 256 + 256, :], write)
    lane_block = iota((64, 256), 1) >> 6
    for k in range(2):
        rows = slots[k]
        rotated = jnp.concatenate(
            [dot(rows[:, c * 256 : c * 256 + 256], diag[k, c]) for c in range(2)], axis=1
        ).astype(BF16)
        score = dot(rotated, rows, 1, 1)
        small = jnp.exp(-jnp.abs(score))
        big_side = 1.0 / (1.0 + small)
        small_side = small * big_side
        sigmoid = jnp.where(score >= 0, big_side, small_side)
        sigmoid_neg = jnp.where(score >= 0, small_side, big_side)
        pairs = jnp.sum(edges[k], axis=1, keepdims=True) * times[k][0:1, :]
        weight = (pairs * sigmoid / neg_count - edges[k] * sigmoid_neg).astype(BF16)
        grad_rotated = dot(weight, rows).astype(BF16)
        grad_other = dot(weight, rotated, 0, 0)
        for c in range(2):
            lanes = slice(c * 256, c * 256 + 256)
            grad_head = dot(grad_rotated[:, lanes], diag[k, c], 1, 1)
            grads[k, :, lanes] = (grad_head + grad_other[:, lanes]).astype(BF16)
            outer = dot(rows[:, lanes], grad_rotated[:, lanes], 0, 0)
            total = jnp.zeros((64, 256), F32)
            for j in range(4):
                total = jnp.where(lane_block == j, outer[64 * j : 64 * j + 64, :], total)
            partial[k, :, lanes] = total

    p = iota((256, 128), 0)
    g = iota((256, 128), 1)
    piece = p & 3
    source = ((p >> 2) & 1) * 64 + piece * 32 + ((p >> 3) & 3) * 8 + (p >> 5)
    spread = onehot((g == source) & (piece < 2))
    named = jnp.where(((p >> 2) & 1) == 0, names[0:1, :], names[1:2, :])

    def write_packed(b, rows):
        out_ref[b * 256 : b * 256 + 256, 0:256] = rows
        rows = jnp.concatenate(
            [
                partial[k, q * 32 + b * 8 : q * 32 + b * 8 + 8, x * 128 : x * 128 + 128]
                for k in range(2)
                for q in range(2)
                for x in range(4)
            ],
            axis=0,
        ).astype(BF16)
        out_ref[b * 256 : b * 256 + 256, 256:384] = jnp.where(piece == 2, named, dot(spread, rows)).astype(BF16)

    pack_slots(lambda k, b: grads[k, b * 64 : b * 64 + 64, :], write_packed)


def relation_kernel(rep_ref, own_ref, keep_ref, give_ref):
    matrix = unpack_matrix()
    lane = iota((128, 128), 1)
    totals = [jnp.zeros((128, 128), F32) for q in range(2)]
    blocks = [dot(matrix, own_ref[b * 256 : b * 256 + 256, :]) for b in range(4)]

    def piece(index):
        return jnp.concatenate([rows[index * 32 : index * 32 + 32] for rows in blocks], axis=0)

    for k in range(2):
        chosen = onehot(lane == piece(4 * k + 2).astype(jnp.int32))
        for q in range(2):
            totals[q] = totals[q] + dot(chosen, piece(4 * k + q).astype(BF16), 0, 0)
    first = rep_ref[0] == 0
    keep_ref[...] = jnp.where(first, totals[0], totals[1])[0:16]
    give_ref[...] = jnp.where(first, totals[1], totals[0])[0:16]


def scatter_kernel(own_ref, peer_ref, own_ids, peer_ids, out_ref, rows_ref):
    @pl.when(pl.program_id(0) == 0)
    def _():
        for r, ref in enumerate((own_ref, peer_ref)):

            def write(k, b, h, rows):
                start = (r * 2 + k) * 256 + b * 64
                rows_ref[start : start + 64, h * 256 : h * 256 + 256] = rows

            unpack_slots(lambda b: ref[b * 256 : b * 256 + 256, :], write)

    base = pl.program_id(0) * 256
    entity = iota((256, 256), 0) + base
    total = jnp.zeros(out_ref.shape, F32)
    for r, ref in enumerate((own_ids, peer_ids)):
        for k in range(2):
            start = (r * 2 + k) * 256
            hit = onehot(entity == ref[k : k + 1, :].astype(jnp.int32))
            total = total + dot(hit, rows_ref[start : start + 256, :])
    out_ref[...] = total


def order_kernel(rows_ref, out_ref):
    g = iota((256, 256), 0)
    p = iota((256, 256), 1)
    matrix = onehot(p == (g & 15) * 16 + (g >> 4))
    for y in range(2):
        out_ref[y * 256 : y * 256 + 256, :] = dot(matrix, rows_ref[y * 256 : y * 256 + 256, :]).astype(BF16)


def widen(piece, result):
    for y in range(2):
        rows = piece[y * 256 : y * 256 + 256, :].astype(F32).reshape(16, 16, 128)
        for side in range(2):
            result[:, side, y * 16 : y * 16 + 16] = rows[:, :, 64 * side : 64 * side + 64]


def widen_kernel(*refs):
    for n, piece in enumerate(refs[:-1]):
        widen(piece, refs[-1].at[n])


def lay_out_kernel(count, ready, xs_ref, qs_ref, *refs):
    pieces = refs[:count]
    out_ref, result, sem = refs[-3:]
    copies = []

    def send(n, source):
        copy = pltpu.make_async_copy(source, out_ref.at[:, xs_ref[n], :, qs_ref[n]], sem.at[n])
        copy.start()
        copies.append(copy)

    for n in range(ready):
        send(count + n, refs[count].at[n])
    for n in range(count):
        widen(pieces[n], result.at[n])
        send(n, result.at[n])
    for copy in copies:
        copy.wait()


def chip(y, z, x):
    return (y * 8 + z) * 4 + x


ACROSS_YZ = [[chip(y, z, x) for y in range(4) for z in range(8)] for x in range(4)]


def along_x(step):
    return [(chip(y, z, x), chip(y, z, (x + step) % 4)) for y in range(4) for z in range(8) for x in range(4)]


def gather_among(rows, groups):
    count = len(groups[0])
    spread = jnp.broadcast_to(rows[None], (count,) + rows.shape)
    out = lax.all_to_all(spread, "bucket", 0, 0, axis_index_groups=groups, tiled=True)
    return out.reshape(count * rows.shape[0], rows.shape[1])


WIDE = (16, 2, 32, 64)


def lay_out(pieces, wide, xs, qs, into):
    view = (16, 4, 2, 2, 32, 64)
    count = len(pieces)
    ready = 0 if wide is None else wide.shape[0]
    arrays = list(pieces) + ([] if wide is None else [wide])
    earlier = [] if into is None else [into]
    scalars = pl.BlockSpec(memory_space=pltpu.SMEM)
    return pl.pallas_call(
        functools.partial(lay_out_kernel, count, ready),
        out_shape=jax.ShapeDtypeStruct(view, F32),
        in_specs=[scalars] * 2 + [VMEM] * len(arrays) + [HBM] * len(earlier),
        out_specs=HBM,
        scratch_shapes=[pltpu.VMEM((count,) + WIDE, F32), pltpu.SemaphoreType.DMA((count + ready,))],
        input_output_aliases={2 + len(arrays): 0} if earlier else {},
        compiler_params=limit(8),
        cost_estimate=pl.CostEstimate(flops=1 << 20, bytes_accessed=count << 20, transcendentals=0),
        name="lay_out_relations",
    )(xs, qs, *arrays, *earlier)


def limit(mib):
    return pltpu.CompilerParams(vmem_limit_bytes=mib << 20)


def body(entity_table, relations, send_rows, send_count, heads, tails, negatives, span_rel):
    entities, width = entity_table.shape
    chips = send_count.shape[3]
    rep = lax.axis_index("rep").astype(jnp.int32).reshape(1)
    swap = [(0, 1), (1, 0)]

    packed, ids = pl.pallas_call(
        send_kernel,
        out_shape=(jax.ShapeDtypeStruct((chips * 8, 256), BF16), jax.ShapeDtypeStruct((8, 256), F32)),
        in_specs=[HBM, HBM, HBM],
        out_specs=(HBM, VMEM),
        scratch_shapes=[
            pltpu.VMEM(send_rows.shape[2:], jnp.int32),
            pltpu.VMEM(send_count.shape[2:], jnp.int32),
            pltpu.VMEM((entities, width), BF16),
            pltpu.VMEM((512, width), BF16),
            pltpu.VMEM((chips * 8, 256), BF16),
            pltpu.SemaphoreType.DMA((2,)),
            pltpu.SemaphoreType.DMA((4,)),
            pltpu.SemaphoreType.DMA((4,)),
        ],
        name="send_rows",
    )(send_rows[0, 0], send_count[0, 0], entity_table)
    peer_ids = lax.ppermute(ids, "rep", swap)

    received = lax.all_to_all(packed.reshape(chips, 8, 256), "bucket", 0, 0, tiled=True).reshape(chips * 8, 256)
    rel_ids = span_rel.reshape(2)
    neg_count = negatives.shape[4]
    used = jnp.concatenate([lax.dynamic_slice_in_dim(relations, rel_ids[k], 1) for k in range(2)])
    shapes = ((8, 128), (2, 2, 256, 256), (2, 256, 256), (2, 8, 256))
    counts = pl.pallas_call(
        count_kernel,
        out_shape=tuple(jax.ShapeDtypeStruct(shape, t) for shape, t in zip(shapes, (F32, BF16, F32, F32))),
        in_specs=[pl.BlockSpec(memory_space=pltpu.SMEM)] + [VMEM] * 4,
        out_specs=(VMEM,) * 4,
        compiler_params=limit(16),
        cost_estimate=pl.CostEstimate(flops=1 << 28, bytes_accessed=4 << 20, transcendentals=0),
        name="count_edges",
    )(rel_ids, used, heads.reshape(2, -1), tails.reshape(2, -1), negatives.reshape(2, -1))

    x = lax.axis_index("bucket").astype(jnp.int32) & 3
    xs = (x - jnp.array([0, 1, 2, 3, 1, 2, 3], jnp.int32)) & 3
    own_q = jnp.broadcast_to(rep, (1,))
    qs = jnp.where(jnp.arange(7) < 4, 1 - rep, rep)
    first_x = xs[:1]
    places = (first_x, own_q, xs, qs)
    received, peer_ids, places, *counts = lax.optimization_barrier((received, peer_ids, places, *counts))
    first_x, own_q, xs, qs = places
    returned = pl.pallas_call(
        functools.partial(step_kernel, neg_count),
        out_shape=jax.ShapeDtypeStruct((chips * 8, 384), BF16),
        in_specs=[VMEM] * 5,
        out_specs=VMEM,
        scratch_shapes=[
            pltpu.VMEM((2, 256, width), BF16),
            pltpu.VMEM((2, 256, width), BF16),
            pltpu.VMEM((2, 64, width), F32),
        ],
        compiler_params=limit(24),
        name="train_step",
    )(received, *counts)

    own = lax.all_to_all(returned.reshape(chips, 8, 384), "bucket", 0, 0, tiled=True).reshape(chips * 8, 384)

    half_sum = jax.ShapeDtypeStruct((16, 128), F32)
    half_spec = pl.BlockSpec((16, 128), lambda i, rep: (0, 0))
    keep, give = pl.pallas_call(
        relation_kernel,
        out_shape=(half_sum, half_sum),
        grid_spec=pltpu.PrefetchScalarGridSpec(
            num_scalar_prefetch=1,
            grid=(1,),
            in_specs=[pl.BlockSpec((chips * 8, 128), lambda i, rep: (0, 2))],
            out_specs=(half_spec, half_spec),
        ),
        compiler_params=limit(16),
        name="sum_relations",
    )(rep, own)
    sums = (keep + lax.ppermute(give, "rep", swap)).astype(BF16)
    column = gather_among(sums, ACROSS_YZ)
    column = pl.pallas_call(
        order_kernel,
        out_shape=jax.ShapeDtypeStruct(column.shape, BF16),
        in_specs=[VMEM],
        out_specs=VMEM,
        compiler_params=limit(8),
        name="order_column",
    )(column)
    pieces = [column] + [lax.ppermute(column, "bucket", along_x(step)) for step in (1, 2, 3)]

    peer = lax.ppermute(own, "rep", swap)
    chunk = 256
    rows_spec = pl.BlockSpec((chips * 8, 256), lambda i: (0, 0))
    ids_spec = pl.BlockSpec((8, 256), lambda i: (0, 0))
    entity_grad = pl.pallas_call(
        scatter_kernel,
        out_shape=jax.ShapeDtypeStruct((entities, width), F32),
        grid=(entities // chunk,),
        in_specs=[rows_spec, rows_spec, ids_spec, ids_spec],
        out_specs=pl.BlockSpec((chunk, width), lambda i: (i, 0)),
        scratch_shapes=[pltpu.VMEM((1024, width), BF16)],
        compiler_params=limit(16),
        cost_estimate=pl.CostEstimate(flops=2 * 1024 * entities * width, bytes_accessed=16 << 20, transcendentals=0),
        name="scatter_rows",
    )(own, peer, ids, peer_ids)

    relation_grad = lay_out(pieces[:1], None, first_x, own_q, None)
    peer_pieces = []
    for n in range(4):
        pieces[n], entity_grad, relation_grad = lax.optimization_barrier((pieces[n], entity_grad, relation_grad))
        peer_pieces.append(lax.ppermute(pieces[n], "rep", swap))
    wide = pl.pallas_call(
        widen_kernel,
        out_shape=jax.ShapeDtypeStruct((3,) + WIDE, F32),
        in_specs=[VMEM] * 3,
        out_specs=VMEM,
        compiler_params=limit(8),
        cost_estimate=pl.CostEstimate(flops=1 << 20, bytes_accessed=3 << 20, transcendentals=0),
        name="widen_own",
    )(*pieces[1:])
    relation_grad = lay_out(peer_pieces, wide, xs, qs, relation_grad)
    relation_grad = relation_grad.reshape(relations.shape)
    return entity_grad, relation_grad


def solution(mesh):
    return jax.shard_map(
        body,
        mesh=mesh,
        in_specs=(
            P("bucket", None),
            P(),
            P("bucket", "rep", None, None),
            P("bucket", "rep", None, None),
            P("bucket", "rep", None, None, None),
            P("bucket", "rep", None, None, None),
            P("bucket", "rep", None, None, None),
            P("bucket", "rep", None, None),
        ),
        out_specs=(P("bucket", None), P()),
        check_vma=False,
    )
```

```python
import functools

import jax
import jax.numpy as jnp
from jax import lax
from jax.experimental import pallas as pl
from jax.experimental.pallas import tpu as pltpu
from jax.sharding import PartitionSpec as P

F32 = jnp.float32
BF16 = jnp.bfloat16
VMEM = pl.BlockSpec(memory_space=pltpu.VMEM)
HBM = pl.BlockSpec(memory_space=pltpu.HBM)


def iota(shape, dim):
    return lax.broadcasted_iota(jnp.int32, shape, dim)


def dot(a, b, ca=1, cb=0):
    return lax.dot_general(a, b, (((ca,), (cb,)), ((), ())), preferred_element_type=F32)


def onehot(mask):
    return jnp.where(mask, 1.0, 0.0).astype(BF16)


def unpack_matrix():
    g = iota((256, 256), 0)
    p = iota((256, 256), 1)
    return onehot(p == (g & 31) * 8 + (g >> 5))


def pack_matrix():
    p = iota((256, 256), 0)
    g = iota((256, 256), 1)
    return onehot(p == (g & 31) * 8 + (g >> 5))


def slot_row(ids):
    return ((ids >> 6) << 6) | ((ids & 1) << 5) | ((ids >> 1) & 31)


def pack_slots(read, write):
    matrix = pack_matrix()
    for b in range(4):
        rows = jnp.concatenate(
            [read(k, b)[:, h * 256 : h * 256 + 256] for h in range(2) for k in range(2)], axis=0
        )
        write(b, dot(matrix, rows).astype(BF16))


def unpack_slots(read, write):
    matrix = unpack_matrix()
    for b in range(4):
        rows = dot(matrix, read(b)).astype(BF16)
        for h in range(2):
            for k in range(2):
                start = h * 128 + k * 64
                write(k, b, h, rows[start : start + 64])


def send_kernel(
    rows_hbm, count_hbm, table_ref, packed_ref, ids_ref, rows_ref, count_ref, table, slots, packed, list_sem, in_sem, out_sem
):
    part = table.shape[0] // 4
    lists = [
        pltpu.make_async_copy(rows_hbm, rows_ref, list_sem.at[0]),
        pltpu.make_async_copy(count_hbm, count_ref, list_sem.at[1]),
    ]
    for copy in lists:
        copy.start()

    def fetch(n):
        rows = pl.ds(n * part, part)
        return pltpu.make_async_copy(table_ref.at[rows], table.at[rows], in_sem.at[n])

    def send(b):
        rows = pl.ds(b * 256, 256)
        return pltpu.make_async_copy(packed.at[rows], packed_ref.at[rows], out_sem.at[b])

    for n in range(4):
        fetch(n).start()
    row = iota((512, 128), 0) & 255
    dest = (row >> 6) * 32 + (row & 31)
    other = iota((512, 128), 1)
    column = (iota((512, 1), 0) >> 5) & 1
    for copy in lists:
        copy.wait()

    def both(ref):
        values = ref[...].astype(F32)
        return jnp.concatenate(
            [jnp.broadcast_to(values[k : k + 1], (256, values.shape[1])) for k in range(2)], axis=0
        )

    counts = both(count_ref)
    start = jnp.sum(jnp.where(other < dest, counts, 0.0), axis=1, keepdims=True)
    count = jnp.sum(jnp.where(other == dest, counts, 0.0), axis=1, keepdims=True)
    position = start.astype(jnp.int32) + column
    ids = jnp.sum(jnp.where(iota((512, 256), 1) == position, both(rows_ref), 0.0), axis=1, keepdims=True)
    ids = jnp.where(column < count.astype(jnp.int32), ids, -1.0)
    wanted = ids.astype(jnp.int32)
    entity = iota((512, part), 1)
    total = jnp.zeros((512, table.shape[1]), F32)
    for n in range(4):
        fetch(n).wait()
        total = total + dot(onehot(entity + n * part == wanted), table[n * part : n * part + part, :])
    slots[...] = total.astype(BF16)
    ids_ref[...] = jnp.zeros_like(ids_ref)
    for k in range(2):
        spread = jnp.broadcast_to(ids[k * 256 : k * 256 + 256], (256, 128))
        ids_ref[k : k + 1, :] = jnp.transpose(spread)[0:1, :]

    def write(b, rows):
        packed[b * 256 : b * 256 + 256, :] = rows
        send(b).start()

    pack_slots(lambda k, b: slots[k * 256 + b * 64 : k * 256 + b * 64 + 64, :], write)
    for b in range(4):
        send(b).wait()


def count_kernel(rel_ref, relation_ref, heads_ref, tails_ref, neg_ref, names_ref, diag_ref, edges_ref, times_ref):
    neg_count = neg_ref.shape[1]
    names_ref[...] = jnp.where(iota((8, 128), 0) == 0, rel_ref[0], rel_ref[1]).astype(F32)
    for k in range(2):
        for c in range(2):
            for j in range(4):
                place = onehot(iota((64, 256), 1) == iota((64, 256), 0) + 64 * j)
                diag_ref[k, c, 64 * j : 64 * j + 64, :] = dot(relation_ref[k, 4 * c + j], place).astype(BF16)
        slot = iota((256, heads_ref.shape[1]), 0)
        at_head = onehot(slot == slot_row(heads_ref[k : k + 1, :]))
        at_tail = onehot(slot == slot_row(tails_ref[k : k + 1, :]))
        edges = dot(at_head, at_tail, 1, 1)
        at_neg = onehot(iota((256, neg_count), 0) == slot_row(neg_ref[k : k + 1, :]))
        edges_ref[k] = edges
        times_ref[k] = dot(jnp.ones((8, neg_count), BF16), at_neg, 1, 1)


def step_kernel(
    neg_count, packed_ref, names, diag, edges, times, out_ref, slots, grads, partial
):
    def write(k, b, h, rows):
        slots[k, b * 64 : b * 64 + 64, h * 256 : h * 256 + 256] = rows

    unpack_slots(lambda b: packed_ref[b * 256 : b * 256 + 256, :], write)
    lane_block = iota((64, 256), 1) >> 6
    for k in range(2):
        rows = slots[k]
        rotated = jnp.concatenate(
            [dot(rows[:, c * 256 : c * 256 + 256], diag[k, c]) for c in range(2)], axis=1
        ).astype(BF16)
        score = dot(rotated, rows, 1, 1)
        small = jnp.exp(-jnp.abs(score))
        big_side = 1.0 / (1.0 + small)
        small_side = small * big_side
        sigmoid = jnp.where(score >= 0, big_side, small_side)
        sigmoid_neg = jnp.where(score >= 0, small_side, big_side)
        pairs = jnp.sum(edges[k], axis=1, keepdims=True) * times[k][0:1, :]
        weight = (pairs * sigmoid / neg_count - edges[k] * sigmoid_neg).astype(BF16)
        grad_rotated = dot(weight, rows).astype(BF16)
        grad_other = dot(weight, rotated, 0, 0)
        for c in range(2):
            lanes = slice(c * 256, c * 256 + 256)
            grad_head = dot(grad_rotated[:, lanes], diag[k, c], 1, 1)
            grads[k, :, lanes] = (grad_head + grad_other[:, lanes]).astype(BF16)
            outer = dot(rows[:, lanes], grad_rotated[:, lanes], 0, 0)
            total = jnp.zeros((64, 256), F32)
            for j in range(4):
                total = jnp.where(lane_block == j, outer[64 * j : 64 * j + 64, :], total)
            partial[k, :, lanes] = total

    p = iota((256, 128), 0)
    g = iota((256, 128), 1)
    piece = p & 3
    source = ((p >> 2) & 1) * 64 + piece * 32 + ((p >> 3) & 3) * 8 + (p >> 5)
    spread = onehot((g == source) & (piece < 2))
    named = jnp.where(((p >> 2) & 1) == 0, names[0:1, :], names[1:2, :])

    def write_packed(b, rows):
        out_ref[b * 256 : b * 256 + 256, 0:256] = rows
        rows = jnp.concatenate(
            [
                partial[k, q * 32 + b * 8 : q * 32 + b * 8 + 8, x * 128 : x * 128 + 128]
                for k in range(2)
                for q in range(2)
                for x in range(4)
            ],
            axis=0,
        ).astype(BF16)
        out_ref[b * 256 : b * 256 + 256, 256:384] = jnp.where(piece == 2, named, dot(spread, rows)).astype(BF16)

    pack_slots(lambda k, b: grads[k, b * 64 : b * 64 + 64, :], write_packed)


def relation_kernel(rep_ref, own_ref, keep_ref, give_ref):
    matrix = unpack_matrix()
    lane = iota((128, 128), 1)
    totals = [jnp.zeros((128, 128), F32) for q in range(2)]
    blocks = [dot(matrix, own_ref[b * 256 : b * 256 + 256, :]) for b in range(4)]

    def piece(index):
        return jnp.concatenate([rows[index * 32 : index * 32 + 32] for rows in blocks], axis=0)

    for k in range(2):
        chosen = onehot(lane == piece(4 * k + 2).astype(jnp.int32))
        for q in range(2):
            totals[q] = totals[q] + dot(chosen, piece(4 * k + q).astype(BF16), 0, 0)
    first = rep_ref[0] == 0
    keep_ref[...] = jnp.where(first, totals[0], totals[1])[0:16]
    give_ref[...] = jnp.where(first, totals[1], totals[0])[0:16]


def scatter_kernel(own_ref, peer_ref, own_ids, peer_ids, out_ref, rows_ref):
    @pl.when(pl.program_id(0) == 0)
    def _():
        for r, ref in enumerate((own_ref, peer_ref)):

            def write(k, b, h, rows):
                start = (r * 2 + k) * 256 + b * 64
                rows_ref[start : start + 64, h * 256 : h * 256 + 256] = rows

            unpack_slots(lambda b: ref[b * 256 : b * 256 + 256, :], write)

    count = out_ref.shape[0]
    entity = iota((count, 256), 0) + pl.program_id(0) * count
    hits = [
        onehot(entity == ref[k : k + 1, :].astype(jnp.int32)) for ref in (own_ids, peer_ids) for k in range(2)
    ]
    out_ref[...] = dot(jnp.concatenate(hits, axis=1), rows_ref[...])


def order_kernel(rows_ref, out_ref):
    g = iota((256, 256), 0)
    p = iota((256, 256), 1)
    matrix = onehot(p == (g & 15) * 16 + (g >> 4))
    for y in range(2):
        out_ref[y * 256 : y * 256 + 256, :] = dot(matrix, rows_ref[y * 256 : y * 256 + 256, :]).astype(BF16)


def widen(piece, result):
    for y in range(2):
        rows = piece[y * 256 : y * 256 + 256, :].astype(F32).reshape(16, 16, 128)
        for side in range(2):
            result[:, side, y * 16 : y * 16 + 16] = rows[:, :, 64 * side : 64 * side + 64]


def widen_kernel(*refs):
    for n, piece in enumerate(refs[:-1]):
        widen(piece, refs[-1].at[n])


def lay_out_kernel(count, ready, xs_ref, qs_ref, *refs):
    pieces = refs[:count]
    out_ref, result, sem = refs[-3:]
    copies = []

    def send(n, source):
        copy = pltpu.make_async_copy(source, out_ref.at[:, xs_ref[n], :, qs_ref[n]], sem.at[n])
        copy.start()
        copies.append(copy)

    for n in range(ready):
        send(count + n, refs[count].at[n])
    for n in range(count):
        widen(pieces[n], result.at[n])
        send(n, result.at[n])
    for copy in copies:
        copy.wait()


def chip(y, z, x):
    return (y * 8 + z) * 4 + x


ACROSS_YZ = [[chip(y, z, x) for y in range(4) for z in range(8)] for x in range(4)]


def along_x(step):
    return [(chip(y, z, x), chip(y, z, (x + step) % 4)) for y in range(4) for z in range(8) for x in range(4)]


def gather_among(rows, groups):
    count = len(groups[0])
    spread = jnp.broadcast_to(rows[None], (count,) + rows.shape)
    out = lax.all_to_all(spread, "bucket", 0, 0, axis_index_groups=groups, tiled=True)
    return out.reshape(count * rows.shape[0], rows.shape[1])


WIDE = (16, 2, 32, 64)


def lay_out(pieces, wide, xs, qs, into):
    view = (16, 4, 2, 2, 32, 64)
    count = len(pieces)
    ready = 0 if wide is None else wide.shape[0]
    arrays = list(pieces) + ([] if wide is None else [wide])
    earlier = [] if into is None else [into]
    scalars = pl.BlockSpec(memory_space=pltpu.SMEM)
    return pl.pallas_call(
        functools.partial(lay_out_kernel, count, ready),
        out_shape=jax.ShapeDtypeStruct(view, F32),
        in_specs=[scalars] * 2 + [VMEM] * len(arrays) + [HBM] * len(earlier),
        out_specs=HBM,
        scratch_shapes=[pltpu.VMEM((count,) + WIDE, F32), pltpu.SemaphoreType.DMA((count + ready,))],
        input_output_aliases={2 + len(arrays): 0} if earlier else {},
        compiler_params=limit(8),
        cost_estimate=pl.CostEstimate(flops=1 << 20, bytes_accessed=count << 20, transcendentals=0),
        name="lay_out_relations",
    )(xs, qs, *arrays, *earlier)


def limit(mib):
    return pltpu.CompilerParams(vmem_limit_bytes=mib << 20)


def body(entity_table, relations, send_rows, send_count, heads, tails, negatives, span_rel):
    entities, width = entity_table.shape
    chips = send_count.shape[3]
    rep = lax.axis_index("rep").astype(jnp.int32).reshape(1)
    swap = [(0, 1), (1, 0)]

    packed, ids = pl.pallas_call(
        send_kernel,
        out_shape=(jax.ShapeDtypeStruct((chips * 8, 256), BF16), jax.ShapeDtypeStruct((8, 256), F32)),
        in_specs=[HBM, HBM, HBM],
        out_specs=(HBM, VMEM),
        scratch_shapes=[
            pltpu.VMEM(send_rows.shape[2:], jnp.int32),
            pltpu.VMEM(send_count.shape[2:], jnp.int32),
            pltpu.VMEM((entities, width), BF16),
            pltpu.VMEM((512, width), BF16),
            pltpu.VMEM((chips * 8, 256), BF16),
            pltpu.SemaphoreType.DMA((2,)),
            pltpu.SemaphoreType.DMA((4,)),
            pltpu.SemaphoreType.DMA((4,)),
        ],
        name="send_rows",
    )(send_rows[0, 0], send_count[0, 0], entity_table)
    peer_ids = lax.ppermute(ids, "rep", swap)

    received = lax.all_to_all(packed.reshape(chips, 8, 256), "bucket", 0, 0, tiled=True).reshape(chips * 8, 256)
    rel_ids = span_rel.reshape(2)
    neg_count = negatives.shape[4]
    used = jnp.concatenate([lax.dynamic_slice_in_dim(relations, rel_ids[k], 1) for k in range(2)])
    shapes = ((8, 128), (2, 2, 256, 256), (2, 256, 256), (2, 8, 256))
    counts = pl.pallas_call(
        count_kernel,
        out_shape=tuple(jax.ShapeDtypeStruct(shape, t) for shape, t in zip(shapes, (F32, BF16, F32, F32))),
        in_specs=[pl.BlockSpec(memory_space=pltpu.SMEM)] + [VMEM] * 4,
        out_specs=(VMEM,) * 4,
        compiler_params=limit(16),
        cost_estimate=pl.CostEstimate(flops=1 << 28, bytes_accessed=4 << 20, transcendentals=0),
        name="count_edges",
    )(rel_ids, used, heads.reshape(2, -1), tails.reshape(2, -1), negatives.reshape(2, -1))

    x = lax.axis_index("bucket").astype(jnp.int32) & 3
    xs = (x - jnp.array([0, 1, 2, 3, 1, 2, 3], jnp.int32)) & 3
    own_q = jnp.broadcast_to(rep, (1,))
    qs = jnp.where(jnp.arange(7) < 4, 1 - rep, rep)
    first_x = xs[:1]
    places = (first_x, own_q, xs, qs)
    received, peer_ids, places, *counts = lax.optimization_barrier((received, peer_ids, places, *counts))
    first_x, own_q, xs, qs = places
    returned = pl.pallas_call(
        functools.partial(step_kernel, neg_count),
        out_shape=jax.ShapeDtypeStruct((chips * 8, 384), BF16),
        in_specs=[VMEM] * 5,
        out_specs=VMEM,
        scratch_shapes=[
            pltpu.VMEM((2, 256, width), BF16),
            pltpu.VMEM((2, 256, width), BF16),
            pltpu.VMEM((2, 64, width), F32),
        ],
        compiler_params=limit(24),
        name="train_step",
    )(received, *counts)

    own = lax.all_to_all(returned.reshape(chips, 8, 384), "bucket", 0, 0, tiled=True).reshape(chips * 8, 384)

    half_sum = jax.ShapeDtypeStruct((16, 128), F32)
    half_spec = pl.BlockSpec((16, 128), lambda i, rep: (0, 0))
    keep, give = pl.pallas_call(
        relation_kernel,
        out_shape=(half_sum, half_sum),
        grid_spec=pltpu.PrefetchScalarGridSpec(
            num_scalar_prefetch=1,
            grid=(1,),
            in_specs=[pl.BlockSpec((chips * 8, 128), lambda i, rep: (0, 2))],
            out_specs=(half_spec, half_spec),
        ),
        compiler_params=limit(16),
        name="sum_relations",
    )(rep, own)
    sums = (keep + lax.ppermute(give, "rep", swap)).astype(BF16)
    column = gather_among(sums, ACROSS_YZ)
    column = pl.pallas_call(
        order_kernel,
        out_shape=jax.ShapeDtypeStruct(column.shape, BF16),
        in_specs=[VMEM],
        out_specs=VMEM,
        compiler_params=limit(8),
        name="order_column",
    )(column)
    pieces = [column] + [lax.ppermute(column, "bucket", along_x(step)) for step in (1, 2, 3)]

    peer = lax.ppermute(own, "rep", swap)
    chunk = 512
    rows_spec = pl.BlockSpec((chips * 8, 256), lambda i: (0, 0))
    ids_spec = pl.BlockSpec((8, 256), lambda i: (0, 0))
    entity_grad = pl.pallas_call(
        scatter_kernel,
        out_shape=jax.ShapeDtypeStruct((entities, width), F32),
        grid=(entities // chunk,),
        in_specs=[rows_spec, rows_spec, ids_spec, ids_spec],
        out_specs=pl.BlockSpec((chunk, width), lambda i: (i, 0)),
        scratch_shapes=[pltpu.VMEM((1024, width), BF16)],
        compiler_params=limit(16),
        cost_estimate=pl.CostEstimate(flops=2 * 1024 * entities * width, bytes_accessed=16 << 20, transcendentals=0),
        name="scatter_rows",
    )(own, peer, ids, peer_ids)

    relation_grad = lay_out(pieces[:1], None, first_x, own_q, None)
    peer_pieces = []
    for n in range(4):
        pieces[n], entity_grad, relation_grad = lax.optimization_barrier((pieces[n], entity_grad, relation_grad))
        peer_pieces.append(lax.ppermute(pieces[n], "rep", swap))
    wide = pl.pallas_call(
        widen_kernel,
        out_shape=jax.ShapeDtypeStruct((3,) + WIDE, F32),
        in_specs=[VMEM] * 3,
        out_specs=VMEM,
        compiler_params=limit(8),
        cost_estimate=pl.CostEstimate(flops=1 << 20, bytes_accessed=3 << 20, transcendentals=0),
        name="widen_own",
    )(*pieces[1:])
    relation_grad = lay_out(peer_pieces, wide, xs, qs, relation_grad)
    relation_grad = relation_grad.reshape(relations.shape)
    return entity_grad, relation_grad


def solution(mesh):
    return jax.shard_map(
        body,
        mesh=mesh,
        in_specs=(
            P("bucket", None),
            P(),
            P("bucket", "rep", None, None),
            P("bucket", "rep", None, None),
            P("bucket", "rep", None, None, None),
            P("bucket", "rep", None, None, None),
            P("bucket", "rep", None, None, None),
            P("bucket", "rep", None, None),
        ),
        out_specs=(P("bucket", None), P()),
        check_vma=False,
    )
```

```python
import functools

import jax
import jax.numpy as jnp
from jax import lax
from jax.experimental import pallas as pl
from jax.experimental.pallas import tpu as pltpu
from jax.sharding import PartitionSpec as P

F32 = jnp.float32
BF16 = jnp.bfloat16
VMEM = pl.BlockSpec(memory_space=pltpu.VMEM)
HBM = pl.BlockSpec(memory_space=pltpu.HBM)


def iota(shape, dim):
    return lax.broadcasted_iota(jnp.int32, shape, dim)


def dot(a, b, ca=1, cb=0):
    return lax.dot_general(a, b, (((ca,), (cb,)), ((), ())), preferred_element_type=F32)


def onehot(mask):
    return jnp.where(mask, 1.0, 0.0).astype(BF16)


def unpack_matrix():
    g = iota((256, 256), 0)
    p = iota((256, 256), 1)
    return onehot(p == (g & 31) * 8 + (g >> 5))


def pack_matrix():
    p = iota((256, 256), 0)
    g = iota((256, 256), 1)
    return onehot(p == (g & 31) * 8 + (g >> 5))


def slot_row(ids):
    return ((ids >> 6) << 6) | ((ids & 1) << 5) | ((ids >> 1) & 31)


def pack_slots(read, write):
    matrix = pack_matrix()
    for b in range(4):
        rows = jnp.concatenate(
            [read(k, b)[:, h * 256 : h * 256 + 256] for h in range(2) for k in range(2)], axis=0
        )
        write(b, dot(matrix, rows).astype(BF16))


def unpack_slots(read, write):
    matrix = unpack_matrix()
    for b in range(4):
        rows = dot(matrix, read(b)).astype(BF16)
        for h in range(2):
            for k in range(2):
                start = h * 128 + k * 64
                write(k, b, h, rows[start : start + 64])


def send_kernel(
    rows_hbm, count_hbm, table_ref, packed_ref, ids_ref, rows_ref, count_ref, table, slots, packed, list_sem, in_sem, out_sem
):
    part = table.shape[0] // 4
    lists = [
        pltpu.make_async_copy(rows_hbm, rows_ref, list_sem.at[0]),
        pltpu.make_async_copy(count_hbm, count_ref, list_sem.at[1]),
    ]
    for copy in lists:
        copy.start()

    def fetch(n):
        rows = pl.ds(n * part, part)
        return pltpu.make_async_copy(table_ref.at[rows], table.at[rows], in_sem.at[n])

    def send(b):
        rows = pl.ds(b * 256, 256)
        return pltpu.make_async_copy(packed.at[rows], packed_ref.at[rows], out_sem.at[b])

    for n in range(4):
        fetch(n).start()
    row = iota((512, 128), 0) & 255
    dest = (row >> 6) * 32 + (row & 31)
    other = iota((512, 128), 1)
    column = (iota((512, 1), 0) >> 5) & 1
    for copy in lists:
        copy.wait()

    def both(ref):
        values = ref[...].astype(F32)
        return jnp.concatenate(
            [jnp.broadcast_to(values[k : k + 1], (256, values.shape[1])) for k in range(2)], axis=0
        )

    counts = both(count_ref)
    start = jnp.sum(jnp.where(other < dest, counts, 0.0), axis=1, keepdims=True)
    count = jnp.sum(jnp.where(other == dest, counts, 0.0), axis=1, keepdims=True)
    position = start.astype(jnp.int32) + column
    ids = jnp.sum(jnp.where(iota((512, 256), 1) == position, both(rows_ref), 0.0), axis=1, keepdims=True)
    ids = jnp.where(column < count.astype(jnp.int32), ids, -1.0)
    wanted = ids.astype(jnp.int32)
    entity = iota((512, part), 1)
    total = jnp.zeros((512, table.shape[1]), F32)
    for n in range(4):
        fetch(n).wait()
        total = total + dot(onehot(entity + n * part == wanted), table[n * part : n * part + part, :])
    slots[...] = total.astype(BF16)
    ids_ref[...] = jnp.zeros_like(ids_ref)
    for k in range(2):
        spread = jnp.broadcast_to(ids[k * 256 : k * 256 + 256], (256, 128))
        ids_ref[k : k + 1, :] = jnp.transpose(spread)[0:1, :]

    def write(b, rows):
        packed[b * 256 : b * 256 + 256, :] = rows
        send(b).start()

    pack_slots(lambda k, b: slots[k * 256 + b * 64 : k * 256 + b * 64 + 64, :], write)
    for b in range(4):
        send(b).wait()


def count_kernel(rel_ref, relation_ref, heads_ref, tails_ref, neg_ref, names_ref, diag_ref, edges_ref, times_ref):
    neg_count = neg_ref.shape[1]
    names_ref[...] = jnp.where(iota((8, 128), 0) == 0, rel_ref[0], rel_ref[1]).astype(F32)
    for k in range(2):
        for c in range(2):
            for j in range(4):
                place = onehot(iota((64, 256), 1) == iota((64, 256), 0) + 64 * j)
                diag_ref[k, c, 64 * j : 64 * j + 64, :] = dot(relation_ref[k, 4 * c + j], place).astype(BF16)
        slot = iota((256, heads_ref.shape[1]), 0)
        at_head = onehot(slot == slot_row(heads_ref[k : k + 1, :]))
        at_tail = onehot(slot == slot_row(tails_ref[k : k + 1, :]))
        edges = dot(at_head, at_tail, 1, 1)
        at_neg = onehot(iota((256, neg_count), 0) == slot_row(neg_ref[k : k + 1, :]))
        edges_ref[k] = edges
        times_ref[k] = dot(jnp.ones((8, neg_count), BF16), at_neg, 1, 1)


def step_kernel(
    neg_count, packed_ref, names, diag, edges, times, out_ref, slots, grads, partial
):
    def write(k, b, h, rows):
        slots[k, b * 64 : b * 64 + 64, h * 256 : h * 256 + 256] = rows

    unpack_slots(lambda b: packed_ref[b * 256 : b * 256 + 256, :], write)
    lane_block = iota((64, 256), 1) >> 6
    for k in range(2):
        rows = slots[k]
        rotated = jnp.concatenate(
            [dot(rows[:, c * 256 : c * 256 + 256], diag[k, c]) for c in range(2)], axis=1
        ).astype(BF16)
        score = dot(rotated, rows, 1, 1)
        small = jnp.exp(-jnp.abs(score))
        big_side = 1.0 / (1.0 + small)
        small_side = small * big_side
        sigmoid = jnp.where(score >= 0, big_side, small_side)
        sigmoid_neg = jnp.where(score >= 0, small_side, big_side)
        pairs = jnp.sum(edges[k], axis=1, keepdims=True) * (times[k][0:1, :] / neg_count)
        weight = (pairs * sigmoid - edges[k] * sigmoid_neg).astype(BF16)
        grad_rotated = dot(weight, rows).astype(BF16)
        grad_other = dot(weight, rotated, 0, 0)
        for c in range(2):
            lanes = slice(c * 256, c * 256 + 256)
            grad_head = dot(grad_rotated[:, lanes], diag[k, c], 1, 1)
            grads[k, :, lanes] = (grad_head + grad_other[:, lanes]).astype(BF16)
            outer = dot(rows[:, lanes], grad_rotated[:, lanes], 0, 0)
            total = jnp.zeros((64, 256), F32)
            for j in range(4):
                total = jnp.where(lane_block == j, outer[64 * j : 64 * j + 64, :], total)
            partial[k, :, lanes] = total

    p = iota((256, 128), 0)
    g = iota((256, 128), 1)
    piece = p & 3
    source = ((p >> 2) & 1) * 64 + piece * 32 + ((p >> 3) & 3) * 8 + (p >> 5)
    spread = onehot((g == source) & (piece < 2))
    named = jnp.where(((p >> 2) & 1) == 0, names[0:1, :], names[1:2, :])

    def write_packed(b, rows):
        out_ref[b * 256 : b * 256 + 256, 0:256] = rows
        rows = jnp.concatenate(
            [
                partial[k, q * 32 + b * 8 : q * 32 + b * 8 + 8, x * 128 : x * 128 + 128]
                for k in range(2)
                for q in range(2)
                for x in range(4)
            ],
            axis=0,
        ).astype(BF16)
        out_ref[b * 256 : b * 256 + 256, 256:384] = jnp.where(piece == 2, named, dot(spread, rows)).astype(BF16)

    pack_slots(lambda k, b: grads[k, b * 64 : b * 64 + 64, :], write_packed)


def relation_kernel(rep_ref, own_ref, keep_ref, give_ref):
    matrix = unpack_matrix()
    lane = iota((128, 128), 1)
    totals = [jnp.zeros((128, 128), F32) for q in range(2)]
    blocks = [dot(matrix, own_ref[b * 256 : b * 256 + 256, :]) for b in range(4)]

    def piece(index):
        return jnp.concatenate([rows[index * 32 : index * 32 + 32] for rows in blocks], axis=0)

    for k in range(2):
        chosen = onehot(lane == piece(4 * k + 2).astype(jnp.int32))
        for q in range(2):
            totals[q] = totals[q] + dot(chosen, piece(4 * k + q).astype(BF16), 0, 0)
    first = rep_ref[0] == 0
    keep_ref[...] = jnp.where(first, totals[0], totals[1])[0:16]
    give_ref[...] = jnp.where(first, totals[1], totals[0])[0:16]


def scatter_kernel(own_ref, peer_ref, own_ids, peer_ids, out_ref, rows_ref):
    @pl.when(pl.program_id(0) == 0)
    def _():
        for r, ref in enumerate((own_ref, peer_ref)):

            def write(k, b, h, rows):
                start = (r * 2 + k) * 256 + b * 64
                rows_ref[start : start + 64, h * 256 : h * 256 + 256] = rows

            unpack_slots(lambda b: ref[b * 256 : b * 256 + 256, :], write)

    count = out_ref.shape[0]
    entity = iota((count, 256), 0) + pl.program_id(0) * count
    hits = [
        onehot(entity == ref[k : k + 1, :].astype(jnp.int32)) for ref in (own_ids, peer_ids) for k in range(2)
    ]
    out_ref[...] = dot(jnp.concatenate(hits, axis=1), rows_ref[...])


def order_kernel(rows_ref, out_ref):
    g = iota((256, 256), 0)
    p = iota((256, 256), 1)
    matrix = onehot(p == (g & 15) * 16 + (g >> 4))
    for y in range(2):
        out_ref[y * 256 : y * 256 + 256, :] = dot(matrix, rows_ref[y * 256 : y * 256 + 256, :]).astype(BF16)


def widen(piece, result):
    for y in range(2):
        rows = piece[y * 256 : y * 256 + 256, :].astype(F32).reshape(16, 16, 128)
        for side in range(2):
            result[:, side, y * 16 : y * 16 + 16] = rows[:, :, 64 * side : 64 * side + 64]


def widen_kernel(*refs):
    for n, piece in enumerate(refs[:-1]):
        widen(piece, refs[-1].at[n])


def lay_out_kernel(count, ready, xs_ref, qs_ref, *refs):
    pieces = refs[:count]
    out_ref, result, sem = refs[-3:]
    copies = []

    def send(n, source):
        copy = pltpu.make_async_copy(source, out_ref.at[:, xs_ref[n], :, qs_ref[n]], sem.at[n])
        copy.start()
        copies.append(copy)

    for n in range(ready):
        send(count + n, refs[count].at[n])
    for n in range(count):
        widen(pieces[n], result.at[n])
        send(n, result.at[n])
    for copy in copies:
        copy.wait()


def chip(y, z, x):
    return (y * 8 + z) * 4 + x


ACROSS_YZ = [[chip(y, z, x) for y in range(4) for z in range(8)] for x in range(4)]


def along_x(step):
    return [(chip(y, z, x), chip(y, z, (x + step) % 4)) for y in range(4) for z in range(8) for x in range(4)]


def gather_among(rows, groups):
    count = len(groups[0])
    spread = jnp.broadcast_to(rows[None], (count,) + rows.shape)
    out = lax.all_to_all(spread, "bucket", 0, 0, axis_index_groups=groups, tiled=True)
    return out.reshape(count * rows.shape[0], rows.shape[1])


WIDE = (16, 2, 32, 64)


def lay_out(pieces, wide, xs, qs, into):
    view = (16, 4, 2, 2, 32, 64)
    count = len(pieces)
    ready = 0 if wide is None else wide.shape[0]
    arrays = list(pieces) + ([] if wide is None else [wide])
    earlier = [] if into is None else [into]
    scalars = pl.BlockSpec(memory_space=pltpu.SMEM)
    return pl.pallas_call(
        functools.partial(lay_out_kernel, count, ready),
        out_shape=jax.ShapeDtypeStruct(view, F32),
        in_specs=[scalars] * 2 + [VMEM] * len(arrays) + [HBM] * len(earlier),
        out_specs=HBM,
        scratch_shapes=[pltpu.VMEM((count,) + WIDE, F32), pltpu.SemaphoreType.DMA((count + ready,))],
        input_output_aliases={2 + len(arrays): 0} if earlier else {},
        compiler_params=limit(8),
        cost_estimate=pl.CostEstimate(flops=1 << 20, bytes_accessed=count << 20, transcendentals=0),
        name="lay_out_relations",
    )(xs, qs, *arrays, *earlier)


def limit(mib):
    return pltpu.CompilerParams(vmem_limit_bytes=mib << 20)


def body(entity_table, relations, send_rows, send_count, heads, tails, negatives, span_rel):
    entities, width = entity_table.shape
    chips = send_count.shape[3]
    rep = lax.axis_index("rep").astype(jnp.int32).reshape(1)
    swap = [(0, 1), (1, 0)]

    packed, ids = pl.pallas_call(
        send_kernel,
        out_shape=(jax.ShapeDtypeStruct((chips * 8, 256), BF16), jax.ShapeDtypeStruct((8, 256), F32)),
        in_specs=[HBM, HBM, HBM],
        out_specs=(HBM, VMEM),
        scratch_shapes=[
            pltpu.VMEM(send_rows.shape[2:], jnp.int32),
            pltpu.VMEM(send_count.shape[2:], jnp.int32),
            pltpu.VMEM((entities, width), BF16),
            pltpu.VMEM((512, width), BF16),
            pltpu.VMEM((chips * 8, 256), BF16),
            pltpu.SemaphoreType.DMA((2,)),
            pltpu.SemaphoreType.DMA((4,)),
            pltpu.SemaphoreType.DMA((4,)),
        ],
        name="send_rows",
    )(send_rows[0, 0], send_count[0, 0], entity_table)
    peer_ids = lax.ppermute(ids, "rep", swap)

    received = lax.all_to_all(packed.reshape(chips, 8, 256), "bucket", 0, 0, tiled=True).reshape(chips * 8, 256)
    rel_ids = span_rel.reshape(2)
    neg_count = negatives.shape[4]
    used = jnp.concatenate([lax.dynamic_slice_in_dim(relations, rel_ids[k], 1) for k in range(2)])
    shapes = ((8, 128), (2, 2, 256, 256), (2, 256, 256), (2, 8, 256))
    counts = pl.pallas_call(
        count_kernel,
        out_shape=tuple(jax.ShapeDtypeStruct(shape, t) for shape, t in zip(shapes, (F32, BF16, F32, F32))),
        in_specs=[pl.BlockSpec(memory_space=pltpu.SMEM)] + [VMEM] * 4,
        out_specs=(VMEM,) * 4,
        compiler_params=limit(16),
        cost_estimate=pl.CostEstimate(flops=1 << 28, bytes_accessed=4 << 20, transcendentals=0),
        name="count_edges",
    )(rel_ids, used, heads.reshape(2, -1), tails.reshape(2, -1), negatives.reshape(2, -1))

    x = lax.axis_index("bucket").astype(jnp.int32) & 3
    xs = (x - jnp.array([0, 1, 2, 3, 1, 2, 3], jnp.int32)) & 3
    own_q = jnp.broadcast_to(rep, (1,))
    qs = jnp.where(jnp.arange(7) < 4, 1 - rep, rep)
    first_x = xs[:1]
    places = (first_x, own_q, xs, qs)
    received, peer_ids, places, *counts = lax.optimization_barrier((received, peer_ids, places, *counts))
    first_x, own_q, xs, qs = places
    returned = pl.pallas_call(
        functools.partial(step_kernel, neg_count),
        out_shape=jax.ShapeDtypeStruct((chips * 8, 384), BF16),
        in_specs=[VMEM] * 5,
        out_specs=VMEM,
        scratch_shapes=[
            pltpu.VMEM((2, 256, width), BF16),
            pltpu.VMEM((2, 256, width), BF16),
            pltpu.VMEM((2, 64, width), F32),
        ],
        compiler_params=limit(24),
        name="train_step",
    )(received, *counts)

    own = lax.all_to_all(returned.reshape(chips, 8, 384), "bucket", 0, 0, tiled=True).reshape(chips * 8, 384)

    half_sum = jax.ShapeDtypeStruct((16, 128), F32)
    half_spec = pl.BlockSpec((16, 128), lambda i, rep: (0, 0))
    keep, give = pl.pallas_call(
        relation_kernel,
        out_shape=(half_sum, half_sum),
        grid_spec=pltpu.PrefetchScalarGridSpec(
            num_scalar_prefetch=1,
            grid=(1,),
            in_specs=[pl.BlockSpec((chips * 8, 128), lambda i, rep: (0, 2))],
            out_specs=(half_spec, half_spec),
        ),
        compiler_params=limit(16),
        name="sum_relations",
    )(rep, own)
    sums = (keep + lax.ppermute(give, "rep", swap)).astype(BF16)
    column = gather_among(sums, ACROSS_YZ)
    column = pl.pallas_call(
        order_kernel,
        out_shape=jax.ShapeDtypeStruct(column.shape, BF16),
        in_specs=[VMEM],
        out_specs=VMEM,
        compiler_params=limit(8),
        name="order_column",
    )(column)
    pieces = [column] + [lax.ppermute(column, "bucket", along_x(step)) for step in (1, 2, 3)]

    peer = lax.ppermute(own, "rep", swap)
    chunk = 512
    rows_spec = pl.BlockSpec((chips * 8, 256), lambda i: (0, 0))
    ids_spec = pl.BlockSpec((8, 256), lambda i: (0, 0))
    entity_grad = pl.pallas_call(
        scatter_kernel,
        out_shape=jax.ShapeDtypeStruct((entities, width), F32),
        grid=(entities // chunk,),
        in_specs=[rows_spec, rows_spec, ids_spec, ids_spec],
        out_specs=pl.BlockSpec((chunk, width), lambda i: (i, 0)),
        scratch_shapes=[pltpu.VMEM((1024, width), BF16)],
        compiler_params=limit(16),
        cost_estimate=pl.CostEstimate(flops=2 * 1024 * entities * width, bytes_accessed=16 << 20, transcendentals=0),
        name="scatter_rows",
    )(own, peer, ids, peer_ids)

    relation_grad = lay_out(pieces[:1], None, first_x, own_q, None)
    peer_pieces = []
    for n in range(4):
        pieces[n], entity_grad, relation_grad = lax.optimization_barrier((pieces[n], entity_grad, relation_grad))
        peer_pieces.append(lax.ppermute(pieces[n], "rep", swap))
    wide = pl.pallas_call(
        widen_kernel,
        out_shape=jax.ShapeDtypeStruct((3,) + WIDE, F32),
        in_specs=[VMEM] * 3,
        out_specs=VMEM,
        compiler_params=limit(8),
        cost_estimate=pl.CostEstimate(flops=1 << 20, bytes_accessed=3 << 20, transcendentals=0),
        name="widen_own",
    )(*pieces[1:])
    relation_grad = lay_out(peer_pieces, wide, xs, qs, relation_grad)
    relation_grad = relation_grad.reshape(relations.shape)
    return entity_grad, relation_grad


def solution(mesh):
    return jax.shard_map(
        body,
        mesh=mesh,
        in_specs=(
            P("bucket", None),
            P(),
            P("bucket", "rep", None, None),
            P("bucket", "rep", None, None),
            P("bucket", "rep", None, None, None),
            P("bucket", "rep", None, None, None),
            P("bucket", "rep", None, None, None),
            P("bucket", "rep", None, None),
        ),
        out_specs=(P("bucket", None), P()),
        check_vma=False,
    )
```
